32 devices in a mesh: group: 2 (over y), head: 4 (over x, core), st: 4 (over z).
Axes of the slice: x: 2, y: 2, z: 4, core: 2. Of those that a mesh axis runs over, the one named last changes fastest.
Arguments:
- qkv_rows: bfloat16 [12288, 3, 3072], P(('group', 'st'), None, 'head'), parts along dimension 0, may hold values from -6 to 6
- out_weight: bfloat16 [3072, 3072], P('head'), may hold values from -0.15625 to 0.15625
- residual: bfloat16 [12288, 3072], P(('group', 'st'), 'head'), parts along dimension 0, may hold values from -3 to 3
- source: int32 [12288], P(('group', 'st')), parts along dimension 0, may hold values from 0 to 6143, as said below
- target: int32 [12288], P(('group', 'st')), parts along dimension 0, may hold values from 0 to 6143, as said below
- window_first: int32 [12288], P(('group', 'st')), parts along dimension 0, may hold values from 0 to 5760, as said below
Outputs:
- layer_out: bfloat16 [12288, 3072], P(('group', 'st'), 'head'), parts along dimension 0
The draws below stay inside these ranges and needn't reach their ends.
There are 2 independent parts, one for each index of `group`. The reference program is written for one: setup_inputs(seed, part) draws one part's arguments, and reference() takes and returns one part's arrays. A program takes and returns all parts, laid end to end along the dimension named above; an argument that names none is the same for every part. Nothing has to cross between parts.
Inputs may be any that keep to these rules, and one draw needn't show every extreme that they name: `source`: A permutation of the tokens that moves aligned tiles of 64 rows whole and in order. Tile t of every st device's shifted rows comes from the st device a fixed offset further along the axis (cyclically), the offset depending on t only; one st device sends at most 6 tiles to one st device, and exactly 6 to one of them. `target`: the inverse of source. `window_first`: windows are runs of whole aligned tiles inside one st device's 1536 shifted rows, of 384 to 1536 rows; in every draw some window fills all 1536 rows of a device.
All inputs are finite; a program needn't handle non-finite values.
Results may differ from the reference program's by a relative error of at most 0.0095.
Values may be sent and summed in bfloat16 or wider, within the bound.
A program may use at most 128 MiB of HBM per device.

```python
import math
import jax
import jax.numpy as jnp
from jax import lax

D = 3072
HEADS = 24
HD = 128
TOK_DEV = 1536
BLK = 64
MINB = 6
TOKENS = 6144
CAP_BLK = 6
N_HEAD = 4
N_ST = 4


def routing(key):
    dev_count = TOKENS // TOK_DEV
    tile_count = TOK_DEV // BLK
    base_key = jax.random.fold_in(key, 7001)
    star_key, others_key, order_key, cut_key, large_key = jax.random.split(base_key, 5)
    star_off = jax.random.randint(star_key, (), 0, dev_count).astype(jnp.int32)
    others = jnp.arange((dev_count - 1) * CAP_BLK, dtype=jnp.int32) // CAP_BLK
    others = others + (others >= star_off).astype(jnp.int32)
    others = jax.random.permutation(others_key, others)
    offsets = jnp.concatenate([jnp.full((CAP_BLK,), star_off, jnp.int32), others])[:tile_count]
    tile_order = jax.random.permutation(order_key, tile_count).astype(jnp.int32)
    device_ids = jnp.arange(dev_count, dtype=jnp.int32)
    src_dev = (device_ids[:, None] + offsets[None, :]) % dev_count
    src_tile = src_dev * tile_count + tile_order[None, :]
    row_ids = jnp.arange(BLK, dtype=jnp.int32)
    source = (src_tile[:, :, None] * BLK + row_ids[None, None, :]).reshape(-1)
    target = jnp.zeros_like(source).at[source].set(jnp.arange(dev_count * tile_count * BLK, dtype=jnp.int32))
    cut_bits = jax.random.randint(cut_key, (dev_count, tile_count), 0, 2).astype(jnp.int32)
    large_dev = jax.random.randint(large_key, (), 0, dev_count - 1).astype(jnp.int32)
    cut_bits = jnp.where(device_ids[:, None] == large_dev, 0, cut_bits)
    tile_ids = jnp.arange(tile_count, dtype=jnp.int32)[None, :]
    last_dev = device_ids[:, None] == dev_count - 1
    quiet = (tile_ids > tile_count - 2 * MINB) & (tile_ids < tile_count - MINB)
    cut_bits = jnp.where(last_dev & quiet, 0, cut_bits)
    cut_bits = jnp.where(last_dev & (tile_ids == tile_count - MINB), 1, cut_bits)

    def walk_tiles(state_pair, step_in):
        run_length, win_first = state_pair
        bit_now, tile_now = step_in
        do_cut = (run_length >= MINB) & (tile_count - tile_now >= MINB) & (bit_now == 1)
        win_first = jnp.where(do_cut, tile_now, win_first)
        run_length = jnp.where(do_cut, 1, run_length + 1)
        return ((run_length, win_first), win_first)
    start_pair = (jnp.zeros((dev_count,), jnp.int32), jnp.zeros((dev_count,), jnp.int32))
    _, tile_firsts = lax.scan(walk_tiles, start_pair, (cut_bits.T, jnp.arange(tile_count, dtype=jnp.int32)))
    tile_firsts = tile_firsts.T
    first_rows = (device_ids[:, None] * tile_count + tile_firsts) * BLK
    window_first = jnp.repeat(first_rows, BLK, axis=1).reshape(-1).astype(jnp.int32)
    return (source, target, window_first)


def draw_source(key, part):
    return routing(key)[0]


def draw_target(key, part):
    return routing(key)[1]


def draw_window_first(key, part):
    return routing(key)[2]


def draw_qkv_rows(key, part):
    source, target, window_first = routing(key)
    feat_cols = HEADS * HD
    value_key = jax.random.fold_in(jax.random.fold_in(key, 7003), 0)
    spread = jnp.array([1.6, 1.6, 1.0], jnp.float32).reshape(1, 3, 1)
    base_rows = jnp.clip(jax.random.normal(value_key, (TOKENS, 3, feat_cols), jnp.float32) * spread, -6.0, 6.0)
    return base_rows[target].astype(jnp.bfloat16)


def strengthened(values, rng, source, target, blocks, factor):
    owner, partner = [(jnp.arange(values.shape[axis_at]) // (values.shape[axis_at] // blocks)).reshape([-1 if axis == axis_at else 1 for axis in range(values.ndim)]) for axis_at in (source, target)]
    chosen = jax.random.permutation(rng, blocks)[partner]
    strong = (owner == chosen) | (owner == (partner + blocks // 2) % blocks)
    return jnp.where(strong, factor * values, values)


def block_levels(own_key, shape, pieces, least, high):
    def one(dim, blocks):
        draws = jax.random.uniform(jax.random.fold_in(jax.random.fold_in(own_key, 6), dim), (blocks,), jnp.float32, least / len(pieces), high / len(pieces))
        return jnp.repeat(jnp.exp(draws), shape[dim] // blocks).reshape((-1,) + (1,) * (len(shape) - dim - 1))

    factor_of = one(*pieces[0])
    for cut in pieces[1:]:
        factor_of = factor_of * one(*cut)
    return factor_of


def scatter_about(own_key, dims, width, reach, pieces=(), held_as=jnp.bfloat16):
    drawn = width * jax.random.normal(own_key, dims, jnp.float32)
    if pieces:
        drawn = drawn * block_levels(own_key, dims, pieces, -0.22, 0.18)
    return jnp.clip(drawn, -reach, reach).astype(held_as)


def gaussian_with(stream_key, extent, deviation, bound, cuts, heavy, kind=jnp.bfloat16):
    entries = deviation * jax.random.normal(stream_key, extent, jnp.float32)
    if cuts:
        entries = entries * block_levels(stream_key, extent, cuts, -0.22, 0.18)
    return jnp.clip(strengthened(entries, jax.random.fold_in(stream_key, 3), *heavy), -bound, bound).astype(kind)


def setup_inputs(seed: int = 0, part: int = 0) -> dict:
    splits = jax.random.split(jax.random.key(seed), 7)
    part_splits = jax.random.split(jax.random.fold_in(splits[6], part), 7)
    qkv_rows = draw_qkv_rows(jax.random.fold_in(jax.random.fold_in(splits[6], part), 71), part)
    out_weight = gaussian_with(splits[1], (HEADS * HD, D), (HEADS * HD) ** -0.5, 0.15625, ((0, 4),), (0, 1, 4, 2.0))
    residual = scatter_about(part_splits[2], (TOKENS, D), 0.5, 3.0, ((0, 4), (1, 4)))
    source = draw_source(jax.random.fold_in(jax.random.fold_in(splits[6], part), 71), part)
    target = draw_target(jax.random.fold_in(jax.random.fold_in(splits[6], part), 71), part)
    window_first = draw_window_first(jax.random.fold_in(jax.random.fold_in(splits[6], part), 71), part)
    return {"qkv_rows": qkv_rows, "out_weight": out_weight, "residual": residual, "source": source, "target": target, "window_first": window_first}


def attend_block(block_rows, block_first):
    row_count = block_rows.shape[0]
    queries = block_rows[:, 0].astype(jnp.float32).reshape(row_count, HEADS, HD)
    key_rows = block_rows[:, 1].astype(jnp.float32).reshape(row_count, HEADS, HD)
    value_rows = block_rows[:, 2].astype(jnp.float32).reshape(row_count, HEADS, HD)
    scores = jnp.einsum('phd,rhd->hpr', queries, key_rows) / math.sqrt(HD)
    same_window = (block_first[:, None] == block_first[None, :])[None]
    scores = jnp.where(same_window, scores, -1e+30)
    row_max = lax.optimization_barrier(jnp.max(scores, axis=2, keepdims=True))
    expo = jnp.where(same_window, jnp.exp(scores - row_max), 0.0)
    denom = lax.optimization_barrier(jnp.sum(expo, axis=2))
    weights = lax.optimization_barrier(expo.astype(jnp.bfloat16)).astype(jnp.float32)
    numer = jnp.einsum('hpr,rhd->hpd', weights, value_rows)
    result = numer / denom[..., None]
    return jnp.transpose(result, (1, 0, 2)).reshape(row_count, HEADS * HD).astype(jnp.bfloat16)

def reference(qkv_rows, out_weight, residual, source, target, window_first):
    shifted = qkv_rows[source]
    blocks = shifted.reshape(N_ST, TOK_DEV, 3, HEADS * HD)
    firsts = window_first.reshape(N_ST, TOK_DEV)
    attended = lax.map(lambda pair: attend_block(pair[0], pair[1]), (blocks, firsts))
    attended = attended.reshape(TOKENS, HEADS * HD)
    attn_home = attended[target]
    group_cols = HEADS * HD // N_HEAD
    columns = attn_home.reshape(TOKENS, N_HEAD, group_cols)
    weight_groups = out_weight.reshape(N_HEAD, group_cols, D)

    def add_group(running, group_id):
        cols_in = lax.dynamic_index_in_dim(columns, group_id, 1, keepdims=False)
        rows_in = lax.dynamic_index_in_dim(weight_groups, group_id, 0, keepdims=False)
        partial_term = jnp.dot(cols_in, rows_in, preferred_element_type=jnp.float32)
        rounded = lax.optimization_barrier(partial_term.astype(jnp.bfloat16))
        return (running + rounded.astype(jnp.float32), None)
    projected, _ = lax.scan(add_group, jnp.zeros((TOKENS, D), jnp.float32), jnp.arange(N_HEAD, dtype=jnp.int32))
    return (residual.astype(jnp.float32) + projected).astype(jnp.bfloat16)
```

```python
import functools
import math

import jax
import jax.numpy as jnp
from jax import lax
from jax.experimental import pallas as pl
from jax.experimental.pallas import tpu as pltpu
from jax.sharding import PartitionSpec as P

HD = 128
BLK = 64
FAR = 16384.0
LAG = 2
MESH = pl.DeviceIdType.MESH


def partner(a, b, n):
    total, bit = 0, 1
    while bit < n:
        total = total + ((a // bit + b // bit) % 2) * bit
        bit *= 2
    return total


def layer_kernel(
    dims,
    src_ref,
    tgt_ref,
    win_ref,
    qkv_ref,
    w_ref,
    res_ref,
    out_ref,
    first,
    rest,
    packed,
    recv,
    home,
    wbuf,
    q_tag,
    k_tag,
    res_buf,
    ret_out,
    ret_in,
    src_s,
    tgt_s,
    win_s,
    order_s,
    block_s,
    slot_s,
    wid_s,
    load_sem,
    idx_sem,
    wl_sem,
    res_sem,
    qs,
    qr,
    rs,
    rr,
    gs,
    gr,
    ws,
    wr,
):
    n_st, n_head, heads, tiles, cap, cols = dims
    rows = cap * BLK
    slots = n_st * cap
    total = n_st * rows
    tok_rows = tiles * BLK
    my_st = lax.axis_index("st")
    my_head = lax.axis_index("head")
    late = n_st - 1
    bits = (tiles - 1).bit_length()

    def st_peer(step):
        return {"st": partner(my_st, step, n_st)}

    def send_kv(j, step):
        part = pl.ds(step * rows, rows)
        return pltpu.make_async_remote_copy(
            src_ref=packed.at[j, pl.ds(1, 2), part, :],
            dst_ref=recv.at[j, pl.ds(1, 2), part, :],
            send_sem=qs.at[j, 1, step - 1],
            recv_sem=qr.at[j, 1, step - 1],
            device_id=st_peer(step),
            device_id_type=MESH,
        )

    def send_q(j, step):
        part = pl.ds(pl.multiple_of(step * rows, rows), rows)
        return pltpu.make_async_remote_copy(
            src_ref=packed.at[j, 0, part, :],
            dst_ref=recv.at[j, 0, part, :],
            send_sem=qs.at[j, 0, step - 1],
            recv_sem=qr.at[j, 0, step - 1],
            device_id=st_peer(step),
            device_id_type=MESH,
        )

    def return_copy(step):
        part = pl.ds(step * cap, cap)
        return pltpu.make_async_remote_copy(
            src_ref=ret_out.at[part],
            dst_ref=ret_in.at[part],
            send_sem=rs.at[step - 1],
            recv_sem=rr.at[step - 1],
            device_id=st_peer(step),
            device_id_type=MESH,
        )

    chips = n_head // 2
    my_chip = my_head // 2
    my_core = lax.rem(my_head, 2)

    def head_of(place):
        chip = lax.rem(my_chip + place // 2, chips)
        core = my_core if place % 2 == 0 else 1 - my_core
        return chip * 2 + core

    def gather_copy(j, block, place):
        return pltpu.make_async_remote_copy(
            src_ref=home.at[block, j * n_head],
            dst_ref=home.at[block, j * n_head + place],
            send_sem=gs.at[j, block, place - 1],
            recv_sem=gr.at[j, block, place - 1],
            device_id={"head": head_of(place)},
            device_id_type=MESH,
        )

    def relay_copy(j, block, place):
        return pltpu.make_async_remote_copy(
            src_ref=home.at[block, j * n_head + place - 1],
            dst_ref=home.at[block, j * n_head + place],
            send_sem=gs.at[j, block, place - 1],
            recv_sem=gr.at[j, block, place - 1],
            device_id={"head": head_of(1)},
            device_id_type=MESH,
        )

    direct = list(range(2, n_head, 2)) + [1]
    relayed = list(range(3, n_head, 2))

    def weight_cols(place):
        return w_ref.at[:, :, pl.ds(pl.multiple_of(head_of(place) * cols, HD), cols)]

    def weight_copy(place):
        return pltpu.make_async_remote_copy(
            src_ref=weight_cols(place),
            dst_ref=wbuf.at[:, pl.ds(place * HD, HD), :],
            send_sem=ws.at[place - 1],
            recv_sem=wr.at[place - 1],
            device_id={"head": head_of(place)},
            device_id_type=MESH,
        )

    own_weight = pltpu.make_async_copy(weight_cols(0), wbuf.at[:, pl.ds(0, HD), :], wl_sem)
    res_load = pltpu.make_async_copy(res_ref, res_buf, res_sem)
    tgt_load = pltpu.make_async_copy(tgt_ref, tgt_s, idx_sem.at[0])
    src_load = pltpu.make_async_copy(src_ref, src_s, idx_sem.at[1])
    win_load = pltpu.make_async_copy(win_ref, win_s, idx_sem.at[2])
    first_load = pltpu.make_async_copy(qkv_ref.at[:, :, :, pl.ds(0, HD)], first, load_sem.at[0])
    rest_load = pltpu.make_async_copy(
        qkv_ref.at[:, :, :, pl.ds(HD, (heads - 1) * HD)], rest, load_sem.at[1]
    )

    tgt_load.start()
    first_load.start()

    barrier = pltpu.get_barrier_semaphore()
    for step in range(1, n_st):
        pl.semaphore_signal(barrier, inc=1, device_id=st_peer(step), device_id_type=MESH)
    for step in range(1, n_head):
        pl.semaphore_signal(barrier, inc=1, device_id={"head": head_of(step)}, device_id_type=MESH)

    rest_load.start()
    src_load.start()
    win_load.start()
    own_weight.start()
    res_load.start()

    tgt_load.wait()

    def list_tiles(step, carry):
        low = partner(my_st, step, n_st) * tok_rows
        found = jnp.int32(0)
        for i in reversed(range(tiles)):
            at = tgt_s[i * BLK]
            found = jnp.where((at >= low) & (at < low + tok_rows), (found << bits) + i, found)
        for r in range(cap):
            order_s[step * cap + r] = (found >> (bits * r)) & ((1 << bits) - 1)
        return carry

    lax.fori_loop(0, n_st, list_tiles, 0)

    def pack_first(s, carry):
        tile = order_s[s]
        at = pl.ds(pl.multiple_of(s * BLK, BLK), BLK)
        for part in range(3):
            packed[0, part, at, :] = first[part, tile]
        return carry

    def pack_rest(j, s):
        tile = order_s[s]
        at = pl.ds(pl.multiple_of(s * BLK, BLK), BLK)
        lanes = pl.ds(pl.multiple_of((j - 1) * HD, HD), HD)
        for part in range(3):
            packed[j, part, at, :] = rest[part, tile, :, lanes]

    across = list(range(n_st - 1, 0, -1))

    first_load.wait()
    pl.semaphore_wait(barrier, n_st + n_head - 2)
    for step in across:
        lax.fori_loop(step * cap, (step + 1) * cap, pack_first, 0)
        send_kv(0, step).start()
        if step != late:
            send_q(0, step).start()

    def own_first(s, carry):
        tile = order_s[s]
        at = pl.ds(pl.multiple_of(s * BLK, BLK), BLK)
        for part in range(3):
            recv[0, part, at, :] = first[part, tile]
        return carry

    lax.fori_loop(0, cap, own_first, 0)
    rest_load.wait()

    def dispatch(j, carry):
        for step in across:

            def body(s, c):
                pack_rest(j, s)
                return c

            lax.fori_loop(step * cap, (step + 1) * cap, body, 0)
            send_kv(j, step).start()
            if step != late:
                send_q(j, step).start()

        def own(s, c):
            tile = order_s[s]
            at = pl.ds(pl.multiple_of(s * BLK, BLK), BLK)
            lanes = pl.ds(pl.multiple_of((j - 1) * HD, HD), HD)
            for part in range(3):
                recv[j, part, at, :] = rest[part, tile, :, lanes]
            return c

        lax.fori_loop(0, cap, own, 0)
        return carry

    lax.fori_loop(1, heads, dispatch, 0)

    def send_late(j, carry):
        send_q(j, late).start()
        return carry

    lax.fori_loop(0, heads, send_late, 0)
    for place in range(1, n_head):
        weight_copy(place).start()

    def block_of(value):
        found = jnp.int32(0)
        for b in range(1, n_st):
            found = found + (value >= b * tok_rows).astype(jnp.int32)
        return found

    def own_slots(i, carry):
        block_s[i] = block_of(tgt_s[i * BLK])
        return carry

    lax.fori_loop(0, tiles, own_slots, 0)

    def send_slots(i, carry):
        mine = block_s[i]
        rank = jnp.int32(0)
        for other in range(tiles):
            rank = rank + ((block_s[other] == mine) & (other < i)).astype(jnp.int32)
        slot_s[i] = partner(my_st, mine, n_st) * cap + jnp.minimum(rank, cap - 1)
        return carry

    lax.fori_loop(0, tiles, send_slots, 0)
    src_load.wait()
    win_load.wait()

    def away_blocks(i, carry):
        block_s[tiles + i] = block_of(src_s[i * BLK])
        return carry

    lax.fori_loop(0, tiles, away_blocks, 0)

    def recv_slots(i, carry):
        mine = block_s[tiles + i]
        rank = jnp.int32(0)
        for other in range(tiles):
            rank = rank + (
                (block_s[tiles + other] == mine) & (src_s[other * BLK] < src_s[i * BLK])
            ).astype(jnp.int32)
        slot_s[tiles + i] = partner(my_st, mine, n_st) * cap + jnp.minimum(rank, cap - 1)
        return carry

    lax.fori_loop(0, tiles, recv_slots, 0)

    def windows(s, carry):
        found = jnp.int32((HD - 1) * BLK) + my_st * tok_rows
        for i in range(tiles):
            found = jnp.where(slot_s[tiles + i] == s, win_s[i * BLK], found)
        wid_s[s] = (found - my_st * tok_rows) >> (BLK.bit_length() - 1)
        return carry

    lax.fori_loop(0, slots, windows, 0)

    lane = lax.broadcasted_iota(jnp.int32, (BLK, HD), 1)

    def tag(s, carry):
        hit = lane == wid_s[s]
        at = pl.ds(pl.multiple_of(s * BLK, BLK), BLK)
        q_tag[at, :] = jnp.where(hit, 1.0, 0.0).astype(jnp.bfloat16)
        k_tag[at, :] = jnp.where(hit, 0.0, -FAR).astype(jnp.bfloat16)
        return carry

    lax.fori_loop(0, slots, tag, 0)
    scale = math.log2(math.e) / math.sqrt(HD)

    def attend(j, step):
        at = pl.ds(pl.multiple_of(step * rows, rows), rows)
        q = jnp.concatenate([recv[j, 0, at, :], q_tag[at, :]], axis=1)
        k = jnp.concatenate([recv[j, 1], k_tag[...]], axis=1)
        v = jnp.concatenate([recv[j, 2], jnp.ones((total, HD), jnp.bfloat16)], axis=1)
        scores = lax.dot_general(q, k, (((1,), (1,)), ((), ())), preferred_element_type=jnp.float32)
        row_max = jnp.max(scores, axis=1, keepdims=True)
        weights = jnp.exp2((scores - row_max) * scale).astype(jnp.bfloat16)
        both = jnp.dot(weights, v, preferred_element_type=jnp.float32)
        home[step, j * n_head] = (both[:, :HD] / both[:, HD:]).astype(jnp.bfloat16)
        for place in direct:
            gather_copy(j, step, place).start()

    def relay(j, block):
        for place in relayed:
            gather_copy(j, block, place - 1).wait_recv()
            relay_copy(j, block, place).start()

    def project(block):
        def finish(j, carry):
            gather_copy(j, block, 1).wait_recv()
            for place in relayed:
                relay_copy(j, block, place).wait_recv()
            return carry

        lax.fori_loop(0, heads, finish, 0)
        left = jnp.concatenate([home[block, i] for i in range(heads * n_head)], axis=1)
        weight = wbuf[...].reshape(heads * n_head * HD, cols)
        term = jnp.dot(left, weight, preferred_element_type=jnp.float32)
        return term.reshape(cap, BLK, cols).astype(jnp.bfloat16)

    early = n_st - 1
    steps = heads * early

    def item(m):
        return m // early, n_st - 2 - m % early

    def attend_early(m, carry):
        j, step = item(m)

        @pl.when(m % early == 0)
        def _():
            for other in range(1, n_st):
                send_kv(j, other).wait_recv()

        @pl.when(step > 0)
        def _():
            send_q(j, step).wait_recv()

        attend(j, step)

        @pl.when(m >= LAG)
        def _():
            relay(*item(m - LAG))

        return carry

    lax.fori_loop(0, steps, attend_early, 0)

    def relay_early(m, carry):
        relay(*item(m))
        return carry

    lax.fori_loop(steps - LAG, steps, relay_early, 0)

    own_weight.wait()
    for place in range(1, n_head):
        weight_copy(place).wait()

    def give(block):
        ret_out[pl.ds(block * cap, cap)] = project(block)
        return_copy(block).start()

    for block in range(n_st - 2, n_st // 2 - 1, -1):
        give(block)

    def attend_late(j, carry):
        send_q(j, late).wait_recv()
        attend(j, late)

        @pl.when(j >= LAG)
        def _():
            relay(j - LAG, late)

        return carry

    lax.fori_loop(0, heads, attend_late, 0)

    def relay_late(j, carry):
        relay(j, late)
        return carry

    lax.fori_loop(max(heads - LAG, 0), heads, relay_late, 0)
    give(late)
    for block in range(n_st // 2 - 1, 0, -1):
        give(block)
    ret_in[pl.ds(0, cap)] = project(0)

    def drain(j, carry):
        for step in range(1, n_st):
            send_q(j, step).wait_send()
            send_kv(j, step).wait_send()
        for block in range(n_st):
            for place in direct:
                gather_copy(j, block, place).wait_send()
            for place in relayed:
                relay_copy(j, block, place).wait_send()
        return carry

    lax.fori_loop(0, heads, drain, 0)
    res_load.wait()
    for step in range(1, n_st):
        return_copy(step).wait()

    def put(t, carry):
        out_ref[t] = (
            res_buf[t].astype(jnp.float32) + ret_in[slot_s[t]].astype(jnp.float32)
        ).astype(jnp.bfloat16)
        return carry

    lax.fori_loop(0, tiles, put, 0)


def on_device(qkv_rows, out_weight, residual, source, target, window_first):
    tok_rows, three_way, feat_cols = qkv_rows.shape
    width = out_weight.shape[1]
    n_st = lax.axis_size("st")
    n_head = lax.axis_size("head")
    heads = feat_cols // HD
    cols = width // n_head
    tiles = tok_rows // BLK
    cap = max(2, (tiles + n_st - 1) // n_st)
    slots = n_st * cap
    total = slots * BLK
    rows = cap * BLK

    dims = (n_st, n_head, heads, tiles, cap, cols)
    bf16 = jnp.bfloat16
    i32 = jnp.int32
    dma = pltpu.SemaphoreType.DMA
    hbm = pl.BlockSpec(memory_space=pl.ANY)
    projected = pl.pallas_call(
        functools.partial(layer_kernel, dims),
        out_shape=jax.ShapeDtypeStruct((tiles, BLK, cols), bf16),
        in_specs=[hbm] * 6,
        out_specs=pl.BlockSpec(memory_space=pltpu.VMEM),
        scratch_shapes=[
            pltpu.VMEM((3, tiles, BLK, HD), bf16),
            pltpu.VMEM((3, tiles, BLK, (heads - 1) * HD), bf16),
            pltpu.VMEM((heads, 3, total, HD), bf16),
            pltpu.VMEM((heads, 3, total, HD), bf16),
            pltpu.VMEM((n_st, heads * n_head, rows, HD), bf16),
            pltpu.VMEM((heads, n_head * HD, cols), bf16),
            pltpu.VMEM((total, HD), bf16),
            pltpu.VMEM((total, HD), bf16),
            pltpu.VMEM((tiles, BLK, cols), bf16),
            pltpu.VMEM((slots, BLK, cols), bf16),
            pltpu.VMEM((slots, BLK, cols), bf16),
            pltpu.SMEM((tok_rows,), i32),
            pltpu.SMEM((tok_rows,), i32),
            pltpu.SMEM((tok_rows,), i32),
            pltpu.SMEM((slots,), i32),
            pltpu.SMEM((2 * tiles,), i32),
            pltpu.SMEM((2 * tiles,), i32),
            pltpu.SMEM((slots,), i32),
            dma((2,)),
            dma((3,)),
            dma,
            dma,
            dma((heads, 2, n_st - 1)),
            dma((heads, 2, n_st - 1)),
            dma((n_st - 1,)),
            dma((n_st - 1,)),
            dma((heads, n_st, n_head - 1)),
            dma((heads, n_st, n_head - 1)),
            dma((n_head - 1,)),
            dma((n_head - 1,)),
        ],
        compiler_params=pltpu.CompilerParams(
            collective_id=0, has_side_effects=True, vmem_limit_bytes=60 * 1024 * 1024
        ),
    )(
        source,
        target,
        window_first,
        jnp.transpose(qkv_rows, (1, 0, 2)).reshape(three_way, tiles, BLK, feat_cols),
        out_weight.reshape(heads, HD, width),
        residual.reshape(tiles, BLK, cols),
    )
    return projected.reshape(tok_rows, cols)


def solution(mesh):
    placed = (
        P(("group", "st"), None, "head"),
        P("head", None),
        P(("group", "st"), "head"),
        P(("group", "st")),
        P(("group", "st")),
        P(("group", "st")),
    )
    return jax.shard_map(
        on_device, mesh=mesh, in_specs=placed, out_specs=P(("group", "st"), "head"), check_vma=False
    )
```

```python
import functools
import math

import jax
import jax.numpy as jnp
from jax import lax
from jax.experimental import pallas as pl
from jax.experimental.pallas import tpu as pltpu
from jax.sharding import PartitionSpec as P

HD = 128
BLK = 64
FAR = 16384.0
LAG = 2
MESH = pl.DeviceIdType.MESH


def partner(a, b, n):
    total, bit = 0, 1
    while bit < n:
        total = total + ((a // bit + b // bit) % 2) * bit
        bit *= 2
    return total


def layer_kernel(
    dims,
    src_ref,
    tgt_ref,
    win_ref,
    qkv_ref,
    w_ref,
    res_ref,
    out_ref,
    first,
    rest,
    packed,
    recv,
    home,
    wbuf,
    q_tag,
    k_tag,
    res_buf,
    ret_out,
    ret_in,
    src_s,
    tgt_s,
    win_s,
    order_s,
    block_s,
    slot_s,
    wid_s,
    load_sem,
    idx_sem,
    wl_sem,
    res_sem,
    qs,
    qr,
    rs,
    rr,
    gs,
    gr,
    ws,
    wr,
):
    n_st, n_head, heads, tiles, cap, cols = dims
    rows = cap * BLK
    slots = n_st * cap
    total = n_st * rows
    tok_rows = tiles * BLK
    my_st = lax.axis_index("st")
    my_head = lax.axis_index("head")
    late = n_st - 1
    bits = (tiles - 1).bit_length()

    def st_peer(step):
        return {"st": partner(my_st, step, n_st)}

    def send_kv(j, step):
        part = pl.ds(step * rows, rows)
        return pltpu.make_async_remote_copy(
            src_ref=packed.at[j, pl.ds(1, 2), part, :],
            dst_ref=recv.at[j, pl.ds(1, 2), part, :],
            send_sem=qs.at[j, 1, step - 1],
            recv_sem=qr.at[j, 1, step - 1],
            device_id=st_peer(step),
            device_id_type=MESH,
        )

    def send_q(j, step):
        part = pl.ds(pl.multiple_of(step * rows, rows), rows)
        return pltpu.make_async_remote_copy(
            src_ref=packed.at[j, 0, part, :],
            dst_ref=recv.at[j, 0, part, :],
            send_sem=qs.at[j, 0, step - 1],
            recv_sem=qr.at[j, 0, step - 1],
            device_id=st_peer(step),
            device_id_type=MESH,
        )

    def return_copy(step):
        part = pl.ds(step * cap, cap)
        return pltpu.make_async_remote_copy(
            src_ref=ret_out.at[part],
            dst_ref=ret_in.at[part],
            send_sem=rs.at[step - 1],
            recv_sem=rr.at[step - 1],
            device_id=st_peer(step),
            device_id_type=MESH,
        )

    chips = n_head // 2
    my_chip = my_head // 2
    my_core = lax.rem(my_head, 2)

    def head_of(place):
        chip = lax.rem(my_chip + place // 2, chips)
        core = my_core if place % 2 == 0 else 1 - my_core
        return chip * 2 + core

    def gather_copy(j, block, place):
        return pltpu.make_async_remote_copy(
            src_ref=home.at[block, j * n_head],
            dst_ref=home.at[block, j * n_head + place],
            send_sem=gs.at[j, block, place - 1],
            recv_sem=gr.at[j, block, place - 1],
            device_id={"head": head_of(place)},
            device_id_type=MESH,
        )

    def relay_copy(j, block, place):
        return pltpu.make_async_remote_copy(
            src_ref=home.at[block, j * n_head + place - 1],
            dst_ref=home.at[block, j * n_head + place],
            send_sem=gs.at[j, block, place - 1],
            recv_sem=gr.at[j, block, place - 1],
            device_id={"head": head_of(1)},
            device_id_type=MESH,
        )

    direct = list(range(2, n_head, 2)) + [1]
    relayed = list(range(3, n_head, 2))

    def weight_cols(place):
        return w_ref.at[:, :, pl.ds(pl.multiple_of(head_of(place) * cols, HD), cols)]

    def weight_copy(place):
        return pltpu.make_async_remote_copy(
            src_ref=weight_cols(place),
            dst_ref=wbuf.at[:, pl.ds(place * HD, HD), :],
            send_sem=ws.at[place - 1],
            recv_sem=wr.at[place - 1],
            device_id={"head": head_of(place)},
            device_id_type=MESH,
        )

    own_weight = pltpu.make_async_copy(weight_cols(0), wbuf.at[:, pl.ds(0, HD), :], wl_sem)
    res_load = pltpu.make_async_copy(res_ref, res_buf, res_sem)
    tgt_load = pltpu.make_async_copy(tgt_ref, tgt_s, idx_sem.at[0])
    src_load = pltpu.make_async_copy(src_ref, src_s, idx_sem.at[1])
    win_load = pltpu.make_async_copy(win_ref, win_s, idx_sem.at[2])
    first_load = pltpu.make_async_copy(qkv_ref.at[:, :, :, pl.ds(0, HD)], first, load_sem.at[0])
    rest_load = pltpu.make_async_copy(
        qkv_ref.at[:, :, :, pl.ds(HD, (heads - 1) * HD)], rest, load_sem.at[1]
    )

    tgt_load.start()
    first_load.start()

    barrier = pltpu.get_barrier_semaphore()
    for step in range(1, n_st):
        pl.semaphore_signal(barrier, inc=1, device_id=st_peer(step), device_id_type=MESH)
    for step in range(1, n_head):
        pl.semaphore_signal(barrier, inc=1, device_id={"head": head_of(step)}, device_id_type=MESH)

    rest_load.start()
    src_load.start()
    win_load.start()
    own_weight.start()
    res_load.start()

    tgt_load.wait()

    def list_tiles(step, carry):
        low = partner(my_st, step, n_st) * tok_rows
        found = jnp.int32(0)
        for i in reversed(range(tiles)):
            at = tgt_s[i * BLK]
            found = jnp.where((at >= low) & (at < low + tok_rows), (found << bits) + i, found)
        for r in range(cap):
            order_s[step * cap + r] = (found >> (bits * r)) & ((1 << bits) - 1)
        return carry

    lax.fori_loop(0, n_st, list_tiles, 0)

    def pack_first(s, carry):
        tile = order_s[s]
        at = pl.ds(pl.multiple_of(s * BLK, BLK), BLK)
        for part in range(3):
            packed[0, part, at, :] = first[part, tile]
        return carry

    def pack_rest(j, s):
        tile = order_s[s]
        at = pl.ds(pl.multiple_of(s * BLK, BLK), BLK)
        lanes = pl.ds(pl.multiple_of((j - 1) * HD, HD), HD)
        for part in range(3):
            packed[j, part, at, :] = rest[part, tile, :, lanes]

    across = list(range(n_st - 1, 0, -1))

    first_load.wait()
    pl.semaphore_wait(barrier, n_st + n_head - 2)
    for step in across:
        lax.fori_loop(step * cap, (step + 1) * cap, pack_first, 0)
        send_kv(0, step).start()
        if step != late:
            send_q(0, step).start()

    def own_first(s, carry):
        tile = order_s[s]
        at = pl.ds(pl.multiple_of(s * BLK, BLK), BLK)
        for part in range(3):
            recv[0, part, at, :] = first[part, tile]
        return carry

    lax.fori_loop(0, cap, own_first, 0)
    rest_load.wait()

    def dispatch(j, carry):
        for step in across:

            def body(s, c):
                pack_rest(j, s)
                return c

            lax.fori_loop(step * cap, (step + 1) * cap, body, 0)
            send_kv(j, step).start()
            if step != late:
                send_q(j, step).start()

        def own(s, c):
            tile = order_s[s]
            at = pl.ds(pl.multiple_of(s * BLK, BLK), BLK)
            lanes = pl.ds(pl.multiple_of((j - 1) * HD, HD), HD)
            for part in range(3):
                recv[j, part, at, :] = rest[part, tile, :, lanes]
            return c

        lax.fori_loop(0, cap, own, 0)
        return carry

    lax.fori_loop(1, heads, dispatch, 0)

    def send_late(j, carry):
        send_q(j, late).start()
        return carry

    lax.fori_loop(0, heads, send_late, 0)
    for place in range(1, n_head):
        weight_copy(place).start()

    def block_of(value):
        found = jnp.int32(0)
        for b in range(1, n_st):
            found = found + (value >= b * tok_rows).astype(jnp.int32)
        return found

    def own_slots(i, carry):
        block_s[i] = block_of(tgt_s[i * BLK])
        return carry

    lax.fori_loop(0, tiles, own_slots, 0)

    def send_slots(i, carry):
        mine = block_s[i]
        rank = jnp.int32(0)
        for other in range(tiles):
            rank = rank + ((block_s[other] == mine) & (other < i)).astype(jnp.int32)
        slot_s[i] = partner(my_st, mine, n_st) * cap + jnp.minimum(rank, cap - 1)
        return carry

    lax.fori_loop(0, tiles, send_slots, 0)
    src_load.wait()
    win_load.wait()

    def away_blocks(i, carry):
        block_s[tiles + i] = block_of(src_s[i * BLK])
        return carry

    lax.fori_loop(0, tiles, away_blocks, 0)

    def recv_slots(i, carry):
        mine = block_s[tiles + i]
        rank = jnp.int32(0)
        for other in range(tiles):
            rank = rank + (
                (block_s[tiles + other] == mine) & (src_s[other * BLK] < src_s[i * BLK])
            ).astype(jnp.int32)
        slot_s[tiles + i] = partner(my_st, mine, n_st) * cap + jnp.minimum(rank, cap - 1)
        return carry

    lax.fori_loop(0, tiles, recv_slots, 0)

    def windows(s, carry):
        found = jnp.int32((HD - 1) * BLK) + my_st * tok_rows
        for i in range(tiles):
            found = jnp.where(slot_s[tiles + i] == s, win_s[i * BLK], found)
        wid_s[s] = (found - my_st * tok_rows) >> (BLK.bit_length() - 1)
        return carry

    lax.fori_loop(0, slots, windows, 0)

    lane = lax.broadcasted_iota(jnp.int32, (BLK, HD), 1)

    def tag(s, carry):
        hit = lane == wid_s[s]
        at = pl.ds(pl.multiple_of(s * BLK, BLK), BLK)
        q_tag[at, :] = jnp.where(hit, 1.0, 0.0).astype(jnp.bfloat16)
        k_tag[at, :] = jnp.where(hit, 0.0, -FAR).astype(jnp.bfloat16)
        return carry

    lax.fori_loop(0, slots, tag, 0)
    scale = math.log2(math.e) / math.sqrt(HD)

    def attend(j, step):
        at = pl.ds(pl.multiple_of(step * rows, rows), rows)
        q = jnp.concatenate([recv[j, 0, at, :], q_tag[at, :]], axis=1)
        k = jnp.concatenate([recv[j, 1], k_tag[...]], axis=1)
        v = jnp.concatenate([recv[j, 2], jnp.ones((total, HD), jnp.bfloat16)], axis=1)
        scores = lax.dot_general(q, k, (((1,), (1,)), ((), ())), preferred_element_type=jnp.float32)
        row_max = jnp.max(scores, axis=1, keepdims=True)
        weights = jnp.exp2((scores - row_max) * scale).astype(jnp.bfloat16)
        both = jnp.dot(weights, v, preferred_element_type=jnp.float32)
        home[step, j * n_head] = (both[:, :HD] / both[:, HD:]).astype(jnp.bfloat16)
        for place in direct:
            gather_copy(j, step, place).start()

    def relay(j, block):
        for place in relayed:
            gather_copy(j, block, place - 1).wait_recv()
            relay_copy(j, block, place).start()

    def project(block):
        def finish(j, carry):
            gather_copy(j, block, 1).wait_recv()
            for place in relayed:
                relay_copy(j, block, place).wait_recv()
            return carry

        lax.fori_loop(0, heads, finish, 0)
        left = jnp.concatenate([home[block, i] for i in range(heads * n_head)], axis=1)
        weight = wbuf[...].reshape(heads * n_head * HD, cols)
        term = jnp.dot(left, weight, preferred_element_type=jnp.float32)
        return term.reshape(cap, BLK, cols).astype(jnp.bfloat16)

    early = n_st - 1
    steps = heads * early

    def item(m):
        return m // early, n_st - 2 - m % early

    def attend_early(m, carry):
        j, step = item(m)

        @pl.when(m % early == 0)
        def _():
            for other in range(1, n_st):
                send_kv(j, other).wait_recv()

        @pl.when(step > 0)
        def _():
            send_q(j, step).wait_recv()

        attend(j, step)

        @pl.when(m >= LAG)
        def _():
            relay(*item(m - LAG))

        return carry

    lax.fori_loop(0, steps, attend_early, 0)

    def relay_early(m, carry):
        relay(*item(m))
        return carry

    lax.fori_loop(steps - LAG, steps, relay_early, 0)

    own_weight.wait()
    for place in range(1, n_head):
        weight_copy(place).wait()

    def give(block):
        ret_out[pl.ds(block * cap, cap)] = project(block)
        return_copy(block).start()

    for block in range(n_st - 2, n_st // 2 - 1, -1):
        give(block)

    def attend_late(j, carry):
        send_q(j, late).wait_recv()
        attend(j, late)

        @pl.when(j >= LAG)
        def _():
            relay(j - LAG, late)

        return carry

    lax.fori_loop(0, heads, attend_late, 0)

    def relay_late(j, carry):
        relay(j, late)
        return carry

    lax.fori_loop(max(heads - LAG, 0), heads, relay_late, 0)
    give(late)
    for block in range(n_st // 2 - 1, 0, -1):
        give(block)
    ret_in[pl.ds(0, cap)] = project(0)

    def drain(j, carry):
        for step in range(1, n_st):
            send_q(j, step).wait_send()
            send_kv(j, step).wait_send()
        for block in range(n_st):
            for place in direct:
                gather_copy(j, block, place).wait_send()
            for place in relayed:
                relay_copy(j, block, place).wait_send()
        return carry

    lax.fori_loop(0, heads, drain, 0)
    res_load.wait()
    for step in range(1, n_st):
        return_copy(step).wait()

    def put(t, carry):
        out_ref[t] = (
            res_buf[t].astype(jnp.float32) + ret_in[slot_s[t]].astype(jnp.float32)
        ).astype(jnp.bfloat16)
        return carry

    lax.fori_loop(0, tiles, put, 0)


def on_device(qkv_rows, out_weight, residual, source, target, window_first):
    tok_rows, three_way, feat_cols = qkv_rows.shape
    width = out_weight.shape[1]
    n_st = lax.axis_size("st")
    n_head = lax.axis_size("head")
    heads = feat_cols // HD
    cols = width // n_head
    tiles = tok_rows // BLK
    cap = max(2, (tiles + n_st - 1) // n_st)
    slots = n_st * cap
    total = slots * BLK
    rows = cap * BLK

    dims = (n_st, n_head, heads, tiles, cap, cols)
    bf16 = jnp.bfloat16
    i32 = jnp.int32
    dma = pltpu.SemaphoreType.DMA
    hbm = pl.BlockSpec(memory_space=pl.ANY)
    projected = pl.pallas_call(
        functools.partial(layer_kernel, dims),
        out_shape=pltpu.VMEM((tiles, BLK, cols), bf16),
        in_specs=[hbm] * 6,
        out_specs=pl.BlockSpec(memory_space=pltpu.VMEM),
        scratch_shapes=[
            pltpu.VMEM((3, tiles, BLK, HD), bf16),
            pltpu.VMEM((3, tiles, BLK, (heads - 1) * HD), bf16),
            pltpu.VMEM((heads, 3, total, HD), bf16),
            pltpu.VMEM((heads, 3, total, HD), bf16),
            pltpu.VMEM((n_st, heads * n_head, rows, HD), bf16),
            pltpu.VMEM((heads, n_head * HD, cols), bf16),
            pltpu.VMEM((total, HD), bf16),
            pltpu.VMEM((total, HD), bf16),
            pltpu.VMEM((tiles, BLK, cols), bf16),
            pltpu.VMEM((slots, BLK, cols), bf16),
            pltpu.VMEM((slots, BLK, cols), bf16),
            pltpu.SMEM((tok_rows,), i32),
            pltpu.SMEM((tok_rows,), i32),
            pltpu.SMEM((tok_rows,), i32),
            pltpu.SMEM((slots,), i32),
            pltpu.SMEM((2 * tiles,), i32),
            pltpu.SMEM((2 * tiles,), i32),
            pltpu.SMEM((slots,), i32),
            dma((2,)),
            dma((3,)),
            dma,
            dma,
            dma((heads, 2, n_st - 1)),
            dma((heads, 2, n_st - 1)),
            dma((n_st - 1,)),
            dma((n_st - 1,)),
            dma((heads, n_st, n_head - 1)),
            dma((heads, n_st, n_head - 1)),
            dma((n_head - 1,)),
            dma((n_head - 1,)),
        ],
        compiler_params=pltpu.CompilerParams(
            collective_id=0, has_side_effects=True, vmem_limit_bytes=60 * 1024 * 1024
        ),
    )(
        source,
        target,
        window_first,
        jnp.transpose(qkv_rows, (1, 0, 2)).reshape(three_way, tiles, BLK, feat_cols),
        out_weight.reshape(heads, HD, width),
        residual.reshape(tiles, BLK, cols),
    )
    return projected.reshape(tok_rows, cols)


def solution(mesh):
    placed = (
        P(("group", "st"), None, "head"),
        P("head", None),
        P(("group", "st"), "head"),
        P(("group", "st")),
        P(("group", "st")),
        P(("group", "st")),
    )
    return jax.shard_map(
        on_device, mesh=mesh, in_specs=placed, out_specs=P(("group", "st"), "head"), check_vma=False
    )
```

```python
import functools
import math

import jax
import jax.numpy as jnp
from jax import lax
from jax.experimental import pallas as pl
from jax.experimental.pallas import tpu as pltpu
from jax.sharding import PartitionSpec as P

HD = 128
BLK = 64
FAR = 16384.0
LAG = 4
MESH = pl.DeviceIdType.MESH


def partner(a, b, n):
    total, bit = 0, 1
    while bit < n:
        total = total + ((a // bit + b // bit) % 2) * bit
        bit *= 2
    return total


def layer_kernel(
    dims,
    src_ref,
    tgt_ref,
    win_ref,
    qkv_ref,
    w_ref,
    res_ref,
    out_ref,
    first,
    rest,
    packed,
    recv,
    home,
    wbuf,
    q_tag,
    k_tag,
    res_buf,
    ret_out,
    ret_in,
    src_s,
    tgt_s,
    win_s,
    order_s,
    block_s,
    slot_s,
    wid_s,
    load_sem,
    idx_sem,
    wl_sem,
    res_sem,
    qs,
    qr,
    rs,
    rr,
    gs,
    gr,
    ws,
    wr,
):
    n_st, n_head, heads, tiles, cap, cols = dims
    rows = cap * BLK
    slots = n_st * cap
    total = n_st * rows
    tok_rows = tiles * BLK
    my_st = lax.axis_index("st")
    my_head = lax.axis_index("head")
    late = n_st - 1
    bits = (tiles - 1).bit_length()

    def st_peer(step):
        return {"st": partner(my_st, step, n_st)}

    def send_kv(j, step):
        part = pl.ds(step * rows, rows)
        return pltpu.make_async_remote_copy(
            src_ref=packed.at[j, pl.ds(1, 2), part, :],
            dst_ref=recv.at[j, pl.ds(1, 2), part, :],
            send_sem=qs.at[j, 1, step - 1],
            recv_sem=qr.at[j, 1, step - 1],
            device_id=st_peer(step),
            device_id_type=MESH,
        )

    def send_q(j, step):
        part = pl.ds(pl.multiple_of(step * rows, rows), rows)
        return pltpu.make_async_remote_copy(
            src_ref=packed.at[j, 0, part, :],
            dst_ref=recv.at[j, 0, part, :],
            send_sem=qs.at[j, 0, step - 1],
            recv_sem=qr.at[j, 0, step - 1],
            device_id=st_peer(step),
            device_id_type=MESH,
        )

    def return_copy(step):
        part = pl.ds(step * cap, cap)
        return pltpu.make_async_remote_copy(
            src_ref=ret_out.at[part],
            dst_ref=ret_in.at[part],
            send_sem=rs.at[step - 1],
            recv_sem=rr.at[step - 1],
            device_id=st_peer(step),
            device_id_type=MESH,
        )

    chips = n_head // 2
    my_chip = my_head // 2
    my_core = lax.rem(my_head, 2)

    def head_of(place):
        chip = lax.rem(my_chip + place // 2, chips)
        core = my_core if place % 2 == 0 else 1 - my_core
        return chip * 2 + core

    def gather_copy(j, block, place):
        return pltpu.make_async_remote_copy(
            src_ref=home.at[block, j * n_head],
            dst_ref=home.at[block, j * n_head + place],
            send_sem=gs.at[j, block, place - 1],
            recv_sem=gr.at[j, block, place - 1],
            device_id={"head": head_of(place)},
            device_id_type=MESH,
        )

    def relay_copy(j, block, place):
        return pltpu.make_async_remote_copy(
            src_ref=home.at[block, j * n_head + place - 1],
            dst_ref=home.at[block, j * n_head + place],
            send_sem=gs.at[j, block, place - 1],
            recv_sem=gr.at[j, block, place - 1],
            device_id={"head": head_of(1)},
            device_id_type=MESH,
        )

    direct = list(range(2, n_head, 2)) + [1]
    relayed = list(range(3, n_head, 2))

    def weight_cols(place):
        return w_ref.at[:, :, pl.ds(pl.multiple_of(head_of(place) * cols, HD), cols)]

    def weight_copy(place):
        return pltpu.make_async_remote_copy(
            src_ref=weight_cols(place),
            dst_ref=wbuf.at[:, pl.ds(place * HD, HD), :],
            send_sem=ws.at[place - 1],
            recv_sem=wr.at[place - 1],
            device_id={"head": head_of(place)},
            device_id_type=MESH,
        )

    own_weight = pltpu.make_async_copy(weight_cols(0), wbuf.at[:, pl.ds(0, HD), :], wl_sem)
    res_load = pltpu.make_async_copy(res_ref, res_buf, res_sem)
    tgt_load = pltpu.make_async_copy(tgt_ref, tgt_s, idx_sem.at[0])
    src_load = pltpu.make_async_copy(src_ref, src_s, idx_sem.at[1])
    win_load = pltpu.make_async_copy(win_ref, win_s, idx_sem.at[2])
    first_load = pltpu.make_async_copy(qkv_ref.at[:, :, :, pl.ds(0, HD)], first, load_sem.at[0])
    rest_load = pltpu.make_async_copy(
        qkv_ref.at[:, :, :, pl.ds(HD, (heads - 1) * HD)], rest, load_sem.at[1]
    )

    tgt_load.start()
    first_load.start()

    barrier = pltpu.get_barrier_semaphore()
    for step in range(1, n_st):
        pl.semaphore_signal(barrier, inc=1, device_id=st_peer(step), device_id_type=MESH)
    for step in range(1, n_head):
        pl.semaphore_signal(barrier, inc=1, device_id={"head": head_of(step)}, device_id_type=MESH)

    rest_load.start()
    src_load.start()
    win_load.start()
    own_weight.start()
    res_load.start()

    tgt_load.wait()

    def list_tiles(step, carry):
        low = partner(my_st, step, n_st) * tok_rows
        found = jnp.int32(0)
        for i in reversed(range(tiles)):
            at = tgt_s[i * BLK]
            found = jnp.where((at >= low) & (at < low + tok_rows), (found << bits) + i, found)
        for r in range(cap):
            order_s[step * cap + r] = (found >> (bits * r)) & ((1 << bits) - 1)
        return carry

    lax.fori_loop(0, n_st, list_tiles, 0)

    def pack_first(s, carry):
        tile = order_s[s]
        at = pl.ds(pl.multiple_of(s * BLK, BLK), BLK)
        for part in range(3):
            packed[0, part, at, :] = first[part, tile]
        return carry

    def pack_rest(j, s):
        tile = order_s[s]
        at = pl.ds(pl.multiple_of(s * BLK, BLK), BLK)
        lanes = pl.ds(pl.multiple_of((j - 1) * HD, HD), HD)
        for part in range(3):
            packed[j, part, at, :] = rest[part, tile, :, lanes]

    across = list(range(n_st - 1, 0, -1))

    first_load.wait()
    pl.semaphore_wait(barrier, n_st + n_head - 2)
    for step in across:
        lax.fori_loop(step * cap, (step + 1) * cap, pack_first, 0)
        send_kv(0, step).start()
        if step != late:
            send_q(0, step).start()

    def own_first(s, carry):
        tile = order_s[s]
        at = pl.ds(pl.multiple_of(s * BLK, BLK), BLK)
        for part in range(3):
            recv[0, part, at, :] = first[part, tile]
        return carry

    lax.fori_loop(0, cap, own_first, 0)
    rest_load.wait()

    def dispatch(j, carry):
        for step in across:

            def body(s, c):
                pack_rest(j, s)
                return c

            lax.fori_loop(step * cap, (step + 1) * cap, body, 0)
            send_kv(j, step).start()
            if step != late:
                send_q(j, step).start()

        def own(s, c):
            tile = order_s[s]
            at = pl.ds(pl.multiple_of(s * BLK, BLK), BLK)
            lanes = pl.ds(pl.multiple_of((j - 1) * HD, HD), HD)
            for part in range(3):
                recv[j, part, at, :] = rest[part, tile, :, lanes]
            return c

        lax.fori_loop(0, cap, own, 0)
        return carry

    lax.fori_loop(1, heads, dispatch, 0)

    def send_late(j, carry):
        send_q(j, late).start()
        return carry

    lax.fori_loop(0, heads, send_late, 0)
    for place in range(1, n_head):
        weight_copy(place).start()

    def block_of(value):
        found = jnp.int32(0)
        for b in range(1, n_st):
            found = found + (value >= b * tok_rows).astype(jnp.int32)
        return found

    def own_slots(i, carry):
        block_s[i] = block_of(tgt_s[i * BLK])
        return carry

    lax.fori_loop(0, tiles, own_slots, 0)

    def send_slots(i, carry):
        mine = block_s[i]
        rank = jnp.int32(0)
        for other in range(tiles):
            rank = rank + ((block_s[other] == mine) & (other < i)).astype(jnp.int32)
        slot_s[i] = partner(my_st, mine, n_st) * cap + jnp.minimum(rank, cap - 1)
        return carry

    lax.fori_loop(0, tiles, send_slots, 0)
    src_load.wait()
    win_load.wait()

    def away_blocks(i, carry):
        block_s[tiles + i] = block_of(src_s[i * BLK])
        return carry

    lax.fori_loop(0, tiles, away_blocks, 0)

    def recv_slots(i, carry):
        mine = block_s[tiles + i]
        rank = jnp.int32(0)
        for other in range(tiles):
            rank = rank + (
                (block_s[tiles + other] == mine) & (src_s[other * BLK] < src_s[i * BLK])
            ).astype(jnp.int32)
        slot_s[tiles + i] = partner(my_st, mine, n_st) * cap + jnp.minimum(rank, cap - 1)
        return carry

    lax.fori_loop(0, tiles, recv_slots, 0)

    def windows(s, carry):
        found = jnp.int32((HD - 1) * BLK) + my_st * tok_rows
        for i in range(tiles):
            found = jnp.where(slot_s[tiles + i] == s, win_s[i * BLK], found)
        wid_s[s] = (found - my_st * tok_rows) >> (BLK.bit_length() - 1)
        return carry

    lax.fori_loop(0, slots, windows, 0)

    lane = lax.broadcasted_iota(jnp.int32, (BLK, HD), 1)

    def tag(s, carry):
        hit = lane == wid_s[s]
        at = pl.ds(pl.multiple_of(s * BLK, BLK), BLK)
        q_tag[at, :] = jnp.where(hit, 1.0, 0.0).astype(jnp.bfloat16)
        k_tag[at, :] = jnp.where(hit, 0.0, -FAR).astype(jnp.bfloat16)
        return carry

    lax.fori_loop(0, slots, tag, 0)
    scale = math.log2(math.e) / math.sqrt(HD)

    def attend(j, step):
        at = pl.ds(pl.multiple_of(step * rows, rows), rows)
        q = jnp.concatenate([recv[j, 0, at, :], q_tag[at, :]], axis=1)
        k = jnp.concatenate([recv[j, 1], k_tag[...]], axis=1)
        v = jnp.concatenate([recv[j, 2], jnp.ones((total, HD), jnp.bfloat16)], axis=1)
        scores = lax.dot_general(q, k, (((1,), (1,)), ((), ())), preferred_element_type=jnp.float32)
        row_max = jnp.max(scores, axis=1, keepdims=True)
        weights = jnp.exp2((scores - row_max) * scale).astype(jnp.bfloat16)
        both = jnp.dot(weights, v, preferred_element_type=jnp.float32)
        home[step, j * n_head] = (both[:, :HD] / both[:, HD:]).astype(jnp.bfloat16)
        for place in direct:
            gather_copy(j, step, place).start()

    def relay(j, block):
        for place in relayed:
            gather_copy(j, block, place - 1).wait_recv()
            relay_copy(j, block, place).start()

    def project(block):
        def finish(j, carry):
            gather_copy(j, block, 1).wait_recv()
            for place in relayed:
                relay_copy(j, block, place).wait_recv()
            return carry

        lax.fori_loop(0, heads, finish, 0)
        left = jnp.concatenate([home[block, i] for i in range(heads * n_head)], axis=1)
        weight = wbuf[...].reshape(heads * n_head * HD, cols)
        term = jnp.dot(left, weight, preferred_element_type=jnp.float32)
        return term.reshape(cap, BLK, cols).astype(jnp.bfloat16)

    early = n_st - 1
    steps = heads * early

    def item(m):
        return m // early, n_st - 2 - m % early

    def attend_early(m, carry):
        j, step = item(m)

        @pl.when(m % early == 0)
        def _():
            for other in range(1, n_st):
                send_kv(j, other).wait_recv()

        @pl.when(step > 0)
        def _():
            send_q(j, step).wait_recv()

        attend(j, step)

        @pl.when(m >= LAG)
        def _():
            relay(*item(m - LAG))

        return carry

    lax.fori_loop(0, steps, attend_early, 0)

    def relay_early(m, carry):
        relay(*item(m))
        return carry

    lax.fori_loop(steps - LAG, steps, relay_early, 0)

    own_weight.wait()
    for place in range(1, n_head):
        weight_copy(place).wait()

    def give(block):
        ret_out[pl.ds(block * cap, cap)] = project(block)
        return_copy(block).start()

    for block in range(n_st - 2, 0, -1):
        give(block)

    def attend_late(j, carry):
        send_q(j, late).wait_recv()
        attend(j, late)

        @pl.when(j >= LAG)
        def _():
            relay(j - LAG, late)

        return carry

    lax.fori_loop(0, heads, attend_late, 0)

    def relay_late(j, carry):
        relay(j, late)
        return carry

    lax.fori_loop(max(heads - LAG, 0), heads, relay_late, 0)
    give(late)
    ret_in[pl.ds(0, cap)] = project(0)

    def drain(j, carry):
        for step in range(1, n_st):
            send_q(j, step).wait_send()
            send_kv(j, step).wait_send()
        for block in range(n_st):
            for place in direct:
                gather_copy(j, block, place).wait_send()
            for place in relayed:
                relay_copy(j, block, place).wait_send()
        return carry

    lax.fori_loop(0, heads, drain, 0)
    res_load.wait()
    for step in range(1, n_st):
        return_copy(step).wait()

    def put(t, carry):
        out_ref[t] = (
            res_buf[t].astype(jnp.float32) + ret_in[slot_s[t]].astype(jnp.float32)
        ).astype(jnp.bfloat16)
        return carry

    lax.fori_loop(0, tiles, put, 0)


def on_device(qkv_rows, out_weight, residual, source, target, window_first):
    tok_rows, three_way, feat_cols = qkv_rows.shape
    width = out_weight.shape[1]
    n_st = lax.axis_size("st")
    n_head = lax.axis_size("head")
    heads = feat_cols // HD
    cols = width // n_head
    tiles = tok_rows // BLK
    cap = max(2, (tiles + n_st - 1) // n_st)
    slots = n_st * cap
    total = slots * BLK
    rows = cap * BLK

    dims = (n_st, n_head, heads, tiles, cap, cols)
    bf16 = jnp.bfloat16
    i32 = jnp.int32
    dma = pltpu.SemaphoreType.DMA
    hbm = pl.BlockSpec(memory_space=pl.ANY)
    projected = pl.pallas_call(
        functools.partial(layer_kernel, dims),
        out_shape=pltpu.VMEM((tiles, BLK, cols), bf16),
        in_specs=[hbm] * 6,
        out_specs=pl.BlockSpec(memory_space=pltpu.VMEM),
        scratch_shapes=[
            pltpu.VMEM((3, tiles, BLK, HD), bf16),
            pltpu.VMEM((3, tiles, BLK, (heads - 1) * HD), bf16),
            pltpu.VMEM((heads, 3, total, HD), bf16),
            pltpu.VMEM((heads, 3, total, HD), bf16),
            pltpu.VMEM((n_st, heads * n_head, rows, HD), bf16),
            pltpu.VMEM((heads, n_head * HD, cols), bf16),
            pltpu.VMEM((total, HD), bf16),
            pltpu.VMEM((total, HD), bf16),
            pltpu.VMEM((tiles, BLK, cols), bf16),
            pltpu.VMEM((slots, BLK, cols), bf16),
            pltpu.VMEM((slots, BLK, cols), bf16),
            pltpu.SMEM((tok_rows,), i32),
            pltpu.SMEM((tok_rows,), i32),
            pltpu.SMEM((tok_rows,), i32),
            pltpu.SMEM((slots,), i32),
            pltpu.SMEM((2 * tiles,), i32),
            pltpu.SMEM((2 * tiles,), i32),
            pltpu.SMEM((slots,), i32),
            dma((2,)),
            dma((3,)),
            dma,
            dma,
            dma((heads, 2, n_st - 1)),
            dma((heads, 2, n_st - 1)),
            dma((n_st - 1,)),
            dma((n_st - 1,)),
            dma((heads, n_st, n_head - 1)),
            dma((heads, n_st, n_head - 1)),
            dma((n_head - 1,)),
            dma((n_head - 1,)),
        ],
        compiler_params=pltpu.CompilerParams(
            collective_id=0, has_side_effects=True, vmem_limit_bytes=60 * 1024 * 1024
        ),
    )(
        source,
        target,
        window_first,
        jnp.transpose(qkv_rows, (1, 0, 2)).reshape(three_way, tiles, BLK, feat_cols),
        out_weight.reshape(heads, HD, width),
        residual.reshape(tiles, BLK, cols),
    )
    return projected.reshape(tok_rows, cols)


def solution(mesh):
    placed = (
        P(("group", "st"), None, "head"),
        P("head", None),
        P(("group", "st"), "head"),
        P(("group", "st")),
        P(("group", "st")),
        P(("group", "st")),
    )
    return jax.shard_map(
        on_device, mesh=mesh, in_specs=placed, out_specs=P(("group", "st"), "head"), check_vma=False
    )
```

```python
import functools
import math

import jax
import jax.numpy as jnp
from jax import lax
from jax.experimental import pallas as pl
from jax.experimental.pallas import tpu as pltpu
from jax.sharding import PartitionSpec as P

HD = 128
BLK = 64
FAR = 16384.0
LAG = 2
MESH = pl.DeviceIdType.MESH


def partner(a, b, n):
    total, bit = 0, 1
    while bit < n:
        total = total + ((a // bit + b // bit) % 2) * bit
        bit *= 2
    return total


def layer_kernel(
    dims,
    src_ref,
    tgt_ref,
    win_ref,
    qkv_ref,
    w_ref,
    res_ref,
    out_ref,
    first,
    rest,
    packed,
    recv,
    home,
    wbuf,
    q_tag,
    k_tag,
    res_buf,
    ret_out,
    ret_in,
    src_s,
    tgt_s,
    win_s,
    order_s,
    block_s,
    slot_s,
    wid_s,
    load_sem,
    idx_sem,
    wl_sem,
    res_sem,
    qs,
    kv_sem,
    early_sem,
    late_sem,
    rs,
    rr,
    gs,
    near_sem,
    far_sem,
    odd_sem,
    ws,
    wr,
):
    n_st, n_head, heads, tiles, cap, cols = dims
    rows = cap * BLK
    slots = n_st * cap
    total = n_st * rows
    tok_rows = tiles * BLK
    my_st = lax.axis_index("st")
    my_head = lax.axis_index("head")
    late = n_st - 1
    bits = (tiles - 1).bit_length()

    def st_peer(step):
        return {"st": partner(my_st, step, n_st)}

    def send_part(refs, sem, step):
        return pltpu.make_async_remote_copy(
            src_ref=refs[0],
            dst_ref=refs[1],
            send_sem=qs,
            recv_sem=sem,
            device_id=st_peer(step),
            device_id_type=MESH,
        )

    def kv_copy(j, step, count=1):
        at = (j, pl.ds(1, 2), pl.ds(step * rows, count * rows))
        return send_part((packed.at[at], recv.at[at]), kv_sem.at[j], step)

    def q_copy(j, step, count=1):
        at = (j, 0, pl.ds(step * rows, count * rows))
        sem = late_sem if step == late else early_sem
        return send_part((packed.at[at], recv.at[at]), sem.at[j], step)

    def away_copy():
        at = (pl.ds(0, heads), pl.ds(0, 3), pl.ds(rows, total - rows))
        return send_part((packed.at[at], recv.at[at]), kv_sem.at[0], 1)

    def return_copy(step, count=1):
        part = pl.ds(step * cap, count * cap)
        return pltpu.make_async_remote_copy(
            src_ref=ret_out.at[part],
            dst_ref=ret_in.at[part],
            send_sem=rs,
            recv_sem=rr,
            device_id=st_peer(step),
            device_id_type=MESH,
        )

    chips = n_head // 2
    my_chip = my_head // 2
    my_core = lax.rem(my_head, 2)

    def head_of(place):
        chip = lax.rem(my_chip + place // 2, chips)
        core = my_core if place % 2 == 0 else 1 - my_core
        return chip * 2 + core

    half = n_head // 2

    def place_at(place):
        return place // 2 + half * (place % 2)

    def head_copy(source, dest, sem, place):
        return pltpu.make_async_remote_copy(
            src_ref=source,
            dst_ref=dest,
            send_sem=gs,
            recv_sem=sem,
            device_id={"head": head_of(place)},
            device_id_type=MESH,
        )

    def gather_copy(j, block, place, sem):
        return head_copy(home.at[block, j, 0], home.at[block, j, place_at(place)], sem, place)

    def relay_copy(j, block, place):
        return head_copy(
            home.at[block, j, place_at(place - 1)],
            home.at[block, j, place_at(place)],
            odd_sem.at[block],
            1,
        )

    def arrived(region, sem):
        head_copy(region, region, sem, 1).wait_recv()


    def weight_cols(place):
        return w_ref.at[:, :, pl.ds(pl.multiple_of(head_of(place) * cols, HD), cols)]

    def weight_copy(place):
        return pltpu.make_async_remote_copy(
            src_ref=weight_cols(place),
            dst_ref=wbuf.at[:, pl.ds(place_at(place) * HD, HD), :],
            send_sem=ws,
            recv_sem=wr,
            device_id={"head": head_of(place)},
            device_id_type=MESH,
        )

    def weights_copy():
        others = wbuf.at[:, pl.ds(HD, (n_head - 1) * HD), :]
        return pltpu.make_async_remote_copy(
            src_ref=others,
            dst_ref=others,
            send_sem=ws,
            recv_sem=wr,
            device_id={"head": head_of(1)},
            device_id_type=MESH,
        )

    own_weight = pltpu.make_async_copy(weight_cols(0), wbuf.at[:, pl.ds(0, HD), :], wl_sem)
    res_load = pltpu.make_async_copy(res_ref, res_buf, res_sem)
    tgt_load = pltpu.make_async_copy(tgt_ref, tgt_s, idx_sem.at[0])
    src_load = pltpu.make_async_copy(src_ref, src_s, idx_sem.at[1])
    win_load = pltpu.make_async_copy(win_ref, win_s, idx_sem.at[2])
    first_load = pltpu.make_async_copy(qkv_ref.at[:, :, :, pl.ds(0, HD)], first, load_sem.at[0])
    rest_load = pltpu.make_async_copy(
        qkv_ref.at[:, :, :, pl.ds(HD, (heads - 1) * HD)], rest, load_sem.at[1]
    )

    tgt_load.start()
    first_load.start()

    barrier = pltpu.get_barrier_semaphore()
    for step in range(1, n_st):
        pl.semaphore_signal(barrier, inc=1, device_id=st_peer(step), device_id_type=MESH)
    for step in range(1, n_head):
        pl.semaphore_signal(barrier, inc=1, device_id={"head": head_of(step)}, device_id_type=MESH)

    rest_load.start()
    src_load.start()
    win_load.start()
    own_weight.start()
    res_load.start()

    tgt_load.wait()

    def list_tiles(step, carry):
        low = partner(my_st, step, n_st) * tok_rows
        found = jnp.int32(0)
        for i in reversed(range(tiles)):
            at = tgt_s[i * BLK]
            found = jnp.where((at >= low) & (at < low + tok_rows), (found << bits) + i, found)
        for r in range(cap):
            order_s[step * cap + r] = (found >> (bits * r)) & ((1 << bits) - 1)
        return carry

    lax.fori_loop(0, n_st, list_tiles, 0)

    def pack_first(s, carry):
        tile = order_s[s]
        at = pl.ds(pl.multiple_of(s * BLK, BLK), BLK)
        for part in range(3):
            packed[0, part, at, :] = first[part, tile]
        return carry

    def pack_rest(j, s):
        tile = order_s[s]
        at = pl.ds(pl.multiple_of(s * BLK, BLK), BLK)
        lanes = pl.ds(pl.multiple_of((j - 1) * HD, HD), HD)
        for part in range(3):
            packed[j, part, at, :] = rest[part, tile, :, lanes]

    across = list(range(n_st - 1, 0, -1))

    first_load.wait()
    pl.semaphore_wait(barrier, n_st + n_head - 2)
    for step in across:
        lax.fori_loop(step * cap, (step + 1) * cap, pack_first, 0)
        kv_copy(0, step).start()
        if step != late:
            q_copy(0, step).start()

    def own_first(s, carry):
        tile = order_s[s]
        at = pl.ds(pl.multiple_of(s * BLK, BLK), BLK)
        for part in range(3):
            recv[0, part, at, :] = first[part, tile]
        return carry

    lax.fori_loop(0, cap, own_first, 0)
    rest_load.wait()

    def dispatch(j, carry):
        for step in across:

            def body(s, c):
                pack_rest(j, s)
                return c

            lax.fori_loop(step * cap, (step + 1) * cap, body, 0)
            kv_copy(j, step).start()
            if step != late:
                q_copy(j, step).start()

        def own(s, c):
            tile = order_s[s]
            at = pl.ds(pl.multiple_of(s * BLK, BLK), BLK)
            lanes = pl.ds(pl.multiple_of((j - 1) * HD, HD), HD)
            for part in range(3):
                recv[j, part, at, :] = rest[part, tile, :, lanes]
            return c

        lax.fori_loop(0, cap, own, 0)
        return carry

    lax.fori_loop(1, heads, dispatch, 0)

    def send_late(j, carry):
        q_copy(j, late).start()
        return carry

    lax.fori_loop(0, heads, send_late, 0)
    for place in range(1, n_head):
        weight_copy(place).start()

    def block_of(value):
        found = jnp.int32(0)
        for b in range(1, n_st):
            found = found + (value >= b * tok_rows).astype(jnp.int32)
        return found

    def own_slots(i, carry):
        block_s[i] = block_of(tgt_s[i * BLK])
        return carry

    lax.fori_loop(0, tiles, own_slots, 0)

    def send_slots(i, carry):
        mine = block_s[i]
        rank = jnp.int32(0)
        for other in range(tiles):
            rank = rank + ((block_s[other] == mine) & (other < i)).astype(jnp.int32)
        slot_s[i] = partner(my_st, mine, n_st) * cap + jnp.minimum(rank, cap - 1)
        return carry

    lax.fori_loop(0, tiles, send_slots, 0)
    src_load.wait()
    win_load.wait()

    def away_blocks(i, carry):
        block_s[tiles + i] = block_of(src_s[i * BLK])
        return carry

    lax.fori_loop(0, tiles, away_blocks, 0)

    def recv_slots(i, carry):
        mine = block_s[tiles + i]
        rank = jnp.int32(0)
        for other in range(tiles):
            rank = rank + (
                (block_s[tiles + other] == mine) & (src_s[other * BLK] < src_s[i * BLK])
            ).astype(jnp.int32)
        slot_s[tiles + i] = partner(my_st, mine, n_st) * cap + jnp.minimum(rank, cap - 1)
        return carry

    lax.fori_loop(0, tiles, recv_slots, 0)

    def windows(s, carry):
        found = jnp.int32((HD - 1) * BLK) + my_st * tok_rows
        for i in range(tiles):
            found = jnp.where(slot_s[tiles + i] == s, win_s[i * BLK], found)
        wid_s[s] = (found - my_st * tok_rows) >> (BLK.bit_length() - 1)
        return carry

    lax.fori_loop(0, slots, windows, 0)

    lane = lax.broadcasted_iota(jnp.int32, (BLK, HD), 1)

    def tag(s, carry):
        hit = lane == wid_s[s]
        at = pl.ds(pl.multiple_of(s * BLK, BLK), BLK)
        q_tag[at, :] = jnp.where(hit, 1.0, 0.0).astype(jnp.bfloat16)
        k_tag[at, :] = jnp.where(hit, 0.0, -FAR).astype(jnp.bfloat16)
        return carry

    lax.fori_loop(0, slots, tag, 0)
    scale = math.log2(math.e) / math.sqrt(HD)

    def attend(j, step):
        at = pl.ds(pl.multiple_of(step * rows, rows), rows)
        q = jnp.concatenate([recv[j, 0, at, :], q_tag[at, :]], axis=1)
        k = jnp.concatenate([recv[j, 1], k_tag[...]], axis=1)
        v = jnp.concatenate([recv[j, 2], jnp.ones((total, HD), jnp.bfloat16)], axis=1)
        scores = lax.dot_general(q, k, (((1,), (1,)), ((), ())), preferred_element_type=jnp.float32)
        row_max = jnp.max(scores, axis=1, keepdims=True)
        weights = jnp.exp2((scores - row_max) * scale).astype(jnp.bfloat16)
        both = jnp.dot(weights, v, preferred_element_type=jnp.float32)
        home[step, j, 0] = (both[:, :HD] / both[:, HD:]).astype(jnp.bfloat16)

    def gather(j, block, sem):
        for place in range(2, n_head, 2):
            gather_copy(j, block, place, sem.at[j]).start()
        gather_copy(j, block, 1, odd_sem.at[block]).start()

    def relay(j, block):
        for place in range(3, n_head, 2):
            relay_copy(j, block, place).start()

    def relay_near(j):
        if half > 1:
            arrived(home.at[pl.ds(0, late), j, pl.ds(1, half - 1)], near_sem.at[j])

        def body(i, carry):
            relay(j, late - 1 - i)
            return carry

        lax.fori_loop(0, late, body, 0)

    def relay_far(j):
        if half > 1:
            arrived(home.at[late, j, pl.ds(1, half - 1)], far_sem.at[j])
        relay(j, late)

    def project(block):
        arrived(home.at[block, :, pl.ds(half, half)], odd_sem.at[block])
        left = jnp.concatenate([home[block, j, p] for j in range(heads) for p in range(n_head)], axis=1)
        weight = wbuf[...].reshape(heads * n_head * HD, cols)
        term = jnp.dot(left, weight, preferred_element_type=jnp.float32)
        return term.reshape(cap, BLK, cols).astype(jnp.bfloat16)

    def attend_early(j, carry):
        kv_copy(j, 1, n_st - 1).wait_recv()
        if late > 1:
            q_copy(j, 1, late - 1).wait_recv()

        def body(i, c):
            attend(j, late - 1 - i)
            gather(j, late - 1 - i, near_sem)
            return c

        lax.fori_loop(0, late, body, 0)

        @pl.when(j >= 1)
        def _():
            relay_near(j - 1)

        return carry

    lax.fori_loop(0, heads, attend_early, 0)
    relay_near(heads - 1)

    own_weight.wait()
    weights_copy().wait()

    def give(block):
        ret_out[pl.ds(block * cap, cap)] = project(block)
        return_copy(block).start()

    for block in range(n_st - 2, 0, -1):
        give(block)

    def attend_late(j, carry):
        q_copy(j, late).wait_recv()
        attend(j, late)
        gather(j, late, far_sem)

        @pl.when(j >= LAG)
        def _():
            relay_far(j - LAG)

        return carry

    lax.fori_loop(0, heads, attend_late, 0)

    def relay_rest(j, carry):
        relay_far(j)
        return carry

    lax.fori_loop(max(heads - LAG, 0), heads, relay_rest, 0)
    give(late)
    ret_in[pl.ds(0, cap)] = project(0)

    away_copy().wait_send()
    others = home.at[:, :, pl.ds(1, n_head - 1)]
    head_copy(others, others, odd_sem.at[0], 1).wait_send()
    res_load.wait()
    return_copy(1, n_st - 1).wait()

    def put(t, carry):
        out_ref[t] = (
            res_buf[t].astype(jnp.float32) + ret_in[slot_s[t]].astype(jnp.float32)
        ).astype(jnp.bfloat16)
        return carry

    lax.fori_loop(0, tiles, put, 0)


def on_device(qkv_rows, out_weight, residual, source, target, window_first):
    tok_rows, three_way, feat_cols = qkv_rows.shape
    width = out_weight.shape[1]
    n_st = lax.axis_size("st")
    n_head = lax.axis_size("head")
    heads = feat_cols // HD
    cols = width // n_head
    tiles = tok_rows // BLK
    cap = max(2, (tiles + n_st - 1) // n_st)
    slots = n_st * cap
    total = slots * BLK
    rows = cap * BLK

    dims = (n_st, n_head, heads, tiles, cap, cols)
    bf16 = jnp.bfloat16
    i32 = jnp.int32
    dma = pltpu.SemaphoreType.DMA
    hbm = pl.BlockSpec(memory_space=pl.ANY)
    projected = pl.pallas_call(
        functools.partial(layer_kernel, dims),
        out_shape=pltpu.VMEM((tiles, BLK, cols), bf16),
        in_specs=[hbm] * 6,
        out_specs=pl.BlockSpec(memory_space=pltpu.VMEM),
        scratch_shapes=[
            pltpu.VMEM((3, tiles, BLK, HD), bf16),
            pltpu.VMEM((3, tiles, BLK, (heads - 1) * HD), bf16),
            pltpu.VMEM((heads, 3, total, HD), bf16),
            pltpu.VMEM((heads, 3, total, HD), bf16),
            pltpu.VMEM((n_st, heads, n_head, rows, HD), bf16),
            pltpu.VMEM((heads, n_head * HD, cols), bf16),
            pltpu.VMEM((total, HD), bf16),
            pltpu.VMEM((total, HD), bf16),
            pltpu.VMEM((tiles, BLK, cols), bf16),
            pltpu.VMEM((slots, BLK, cols), bf16),
            pltpu.VMEM((slots, BLK, cols), bf16),
            pltpu.SMEM((tok_rows,), i32),
            pltpu.SMEM((tok_rows,), i32),
            pltpu.SMEM((tok_rows,), i32),
            pltpu.SMEM((slots,), i32),
            pltpu.SMEM((2 * tiles,), i32),
            pltpu.SMEM((2 * tiles,), i32),
            pltpu.SMEM((slots,), i32),
            dma((2,)),
            dma((3,)),
            dma,
            dma,
            dma,
            dma((heads,)),
            dma((heads,)),
            dma((heads,)),
            dma,
            dma,
            dma,
            dma((heads,)),
            dma((heads,)),
            dma((n_st,)),
            dma,
            dma,
        ],
        compiler_params=pltpu.CompilerParams(
            collective_id=0, has_side_effects=True, vmem_limit_bytes=60 * 1024 * 1024
        ),
    )(
        source,
        target,
        window_first,
        jnp.transpose(qkv_rows, (1, 0, 2)).reshape(three_way, tiles, BLK, feat_cols),
        out_weight.reshape(heads, HD, width),
        residual.reshape(tiles, BLK, cols),
    )
    return projected.reshape(tok_rows, cols)


def solution(mesh):
    placed = (
        P(("group", "st"), None, "head"),
        P("head", None),
        P(("group", "st"), "head"),
        P(("group", "st")),
        P(("group", "st")),
        P(("group", "st")),
    )
    return jax.shard_map(
        on_device, mesh=mesh, in_specs=placed, out_specs=P(("group", "st"), "head"), check_vma=False
    )
```

```python
import functools
import math

import jax
import jax.numpy as jnp
from jax import lax
from jax.experimental import pallas as pl
from jax.experimental.pallas import tpu as pltpu
from jax.sharding import PartitionSpec as P

HD = 128
BLK = 64
FAR = 16384.0
LAG = 2
MESH = pl.DeviceIdType.MESH


def partner(a, b, n):
    total, bit = 0, 1
    while bit < n:
        total = total + ((a // bit + b // bit) % 2) * bit
        bit *= 2
    return total


def layer_kernel(
    dims,
    src_ref,
    tgt_ref,
    win_ref,
    qkv_ref,
    w_ref,
    res_ref,
    out_ref,
    first,
    rest,
    packed,
    recv,
    home,
    wbuf,
    q_tag,
    k_tag,
    res_buf,
    ret_out,
    ret_in,
    src_s,
    tgt_s,
    win_s,
    order_s,
    block_s,
    slot_s,
    wid_s,
    load_sem,
    idx_sem,
    wl_sem,
    res_sem,
    qs,
    kv_sem,
    early_sem,
    late_sem,
    rs,
    rr,
    gs,
    near_sem,
    far_sem,
    odd_sem,
    ws,
    wr,
):
    n_st, n_head, heads, tiles, cap, cols = dims
    rows = cap * BLK
    slots = n_st * cap
    total = n_st * rows
    tok_rows = tiles * BLK
    my_st = lax.axis_index("st")
    my_head = lax.axis_index("head")
    late = n_st - 1
    bits = (tiles - 1).bit_length()

    def st_peer(step):
        return {"st": partner(my_st, step, n_st)}

    def send_part(refs, sem, step):
        return pltpu.make_async_remote_copy(
            src_ref=refs[0],
            dst_ref=refs[1],
            send_sem=qs,
            recv_sem=sem,
            device_id=st_peer(step),
            device_id_type=MESH,
        )

    def kv_copy(j, step, count=1):
        at = (j, pl.ds(1, 2), pl.ds(step * rows, count * rows))
        return send_part((packed.at[at], recv.at[at]), kv_sem.at[j], step)

    def q_copy(j, step, count=1):
        at = (j, 0, pl.ds(step * rows, count * rows))
        sem = late_sem if step == late else early_sem
        return send_part((packed.at[at], recv.at[at]), sem.at[j], step)

    def away_copy():
        at = (pl.ds(0, heads), pl.ds(0, 3), pl.ds(rows, total - rows))
        return send_part((packed.at[at], recv.at[at]), kv_sem.at[0], 1)

    def return_copy(step, count=1):
        part = pl.ds(step * cap, count * cap)
        return pltpu.make_async_remote_copy(
            src_ref=ret_out.at[part],
            dst_ref=ret_in.at[part],
            send_sem=rs,
            recv_sem=rr,
            device_id=st_peer(step),
            device_id_type=MESH,
        )

    chips = n_head // 2
    my_chip = my_head // 2
    my_core = lax.rem(my_head, 2)

    def head_of(place):
        chip = lax.rem(my_chip + place // 2, chips)
        core = my_core if place % 2 == 0 else 1 - my_core
        return chip * 2 + core

    half = n_head // 2

    def place_at(place):
        return place // 2 + half * (place % 2)

    def head_copy(source, dest, sem, place):
        return pltpu.make_async_remote_copy(
            src_ref=source,
            dst_ref=dest,
            send_sem=gs,
            recv_sem=sem,
            device_id={"head": head_of(place)},
            device_id_type=MESH,
        )

    def gather_copy(j, block, place, sem):
        return head_copy(home.at[block, j, 0], home.at[block, j, place_at(place)], sem, place)

    def relay_copy(j, block, place):
        return head_copy(
            home.at[block, j, place_at(place - 1)],
            home.at[block, j, place_at(place)],
            odd_sem.at[block],
            1,
        )

    def arrived(region, sem):
        head_copy(region, region, sem, 1).wait_recv()


    def weight_cols(place):
        return w_ref.at[:, :, pl.ds(pl.multiple_of(head_of(place) * cols, HD), cols)]

    def weight_copy(place):
        return pltpu.make_async_remote_copy(
            src_ref=weight_cols(place),
            dst_ref=wbuf.at[:, pl.ds(place_at(place) * HD, HD), :],
            send_sem=ws,
            recv_sem=wr,
            device_id={"head": head_of(place)},
            device_id_type=MESH,
        )

    def weights_copy():
        others = wbuf.at[:, pl.ds(HD, (n_head - 1) * HD), :]
        return pltpu.make_async_remote_copy(
            src_ref=others,
            dst_ref=others,
            send_sem=ws,
            recv_sem=wr,
            device_id={"head": head_of(1)},
            device_id_type=MESH,
        )

    own_weight = pltpu.make_async_copy(weight_cols(0), wbuf.at[:, pl.ds(0, HD), :], wl_sem)
    res_load = pltpu.make_async_copy(res_ref, res_buf, res_sem)
    tgt_load = pltpu.make_async_copy(tgt_ref, tgt_s, idx_sem.at[0])
    src_load = pltpu.make_async_copy(src_ref, src_s, idx_sem.at[1])
    win_load = pltpu.make_async_copy(win_ref, win_s, idx_sem.at[2])
    first_load = pltpu.make_async_copy(qkv_ref.at[:, :, :, pl.ds(0, HD)], first, load_sem.at[0])
    rest_load = pltpu.make_async_copy(
        qkv_ref.at[:, :, :, pl.ds(HD, (heads - 1) * HD)], rest, load_sem.at[1]
    )

    tgt_load.start()
    first_load.start()

    barrier = pltpu.get_barrier_semaphore()
    for step in range(1, n_st):
        pl.semaphore_signal(barrier, inc=1, device_id=st_peer(step), device_id_type=MESH)
    for step in range(1, n_head):
        pl.semaphore_signal(barrier, inc=1, device_id={"head": head_of(step)}, device_id_type=MESH)

    rest_load.start()
    src_load.start()
    win_load.start()
    own_weight.start()
    res_load.start()

    tgt_load.wait()

    def list_tiles(step, carry):
        low = partner(my_st, step, n_st) * tok_rows
        found = jnp.int32(0)
        for i in reversed(range(tiles)):
            at = tgt_s[i * BLK]
            found = jnp.where((at >= low) & (at < low + tok_rows), (found << bits) + i, found)
        for r in range(cap):
            order_s[step * cap + r] = (found >> (bits * r)) & ((1 << bits) - 1)
        return carry

    lax.fori_loop(0, n_st, list_tiles, 0)

    def pack_first(s, carry):
        tile = order_s[s]
        at = pl.ds(pl.multiple_of(s * BLK, BLK), BLK)
        for part in range(3):
            packed[0, part, at, :] = first[part, tile]
        return carry

    def pack_rest(j, s):
        tile = order_s[s]
        at = pl.ds(pl.multiple_of(s * BLK, BLK), BLK)
        lanes = pl.ds(pl.multiple_of((j - 1) * HD, HD), HD)
        for part in range(3):
            packed[j, part, at, :] = rest[part, tile, :, lanes]

    across = list(range(n_st - 1, 0, -1))

    first_load.wait()
    pl.semaphore_wait(barrier, n_st + n_head - 2)
    for step in across:
        lax.fori_loop(step * cap, (step + 1) * cap, pack_first, 0)
        kv_copy(0, step).start()
        if step != late:
            q_copy(0, step).start()

    def own_first(s, carry):
        tile = order_s[s]
        at = pl.ds(pl.multiple_of(s * BLK, BLK), BLK)
        for part in range(3):
            recv[0, part, at, :] = first[part, tile]
        return carry

    lax.fori_loop(0, cap, own_first, 0)
    rest_load.wait()

    def dispatch(j, carry):
        for step in across:

            def body(s, c):
                pack_rest(j, s)
                return c

            lax.fori_loop(step * cap, (step + 1) * cap, body, 0)
            kv_copy(j, step).start()
            if step != late:
                q_copy(j, step).start()

        def own(s, c):
            tile = order_s[s]
            at = pl.ds(pl.multiple_of(s * BLK, BLK), BLK)
            lanes = pl.ds(pl.multiple_of((j - 1) * HD, HD), HD)
            for part in range(3):
                recv[j, part, at, :] = rest[part, tile, :, lanes]
            return c

        lax.fori_loop(0, cap, own, 0)
        return carry

    lax.fori_loop(1, heads, dispatch, 0)

    def send_late(j, carry):
        q_copy(j, late).start()
        return carry

    lax.fori_loop(0, heads, send_late, 0)
    for place in range(1, n_head):
        weight_copy(place).start()

    def block_of(value):
        found = jnp.int32(0)
        for b in range(1, n_st):
            found = found + (value >= b * tok_rows).astype(jnp.int32)
        return found

    def own_slots(i, carry):
        block_s[i] = block_of(tgt_s[i * BLK])
        return carry

    lax.fori_loop(0, tiles, own_slots, 0)

    def send_slots(i, carry):
        mine = block_s[i]
        rank = jnp.int32(0)
        for other in range(tiles):
            rank = rank + ((block_s[other] == mine) & (other < i)).astype(jnp.int32)
        slot_s[i] = partner(my_st, mine, n_st) * cap + jnp.minimum(rank, cap - 1)
        return carry

    lax.fori_loop(0, tiles, send_slots, 0)
    src_load.wait()
    win_load.wait()

    def away_blocks(i, carry):
        block_s[tiles + i] = block_of(src_s[i * BLK])
        return carry

    lax.fori_loop(0, tiles, away_blocks, 0)

    def recv_slots(i, carry):
        mine = block_s[tiles + i]
        rank = jnp.int32(0)
        for other in range(tiles):
            rank = rank + (
                (block_s[tiles + other] == mine) & (src_s[other * BLK] < src_s[i * BLK])
            ).astype(jnp.int32)
        slot_s[tiles + i] = partner(my_st, mine, n_st) * cap + jnp.minimum(rank, cap - 1)
        return carry

    lax.fori_loop(0, tiles, recv_slots, 0)

    def windows(s, carry):
        found = jnp.int32((HD - 1) * BLK) + my_st * tok_rows
        for i in range(tiles):
            found = jnp.where(slot_s[tiles + i] == s, win_s[i * BLK], found)
        wid_s[s] = (found - my_st * tok_rows) >> (BLK.bit_length() - 1)
        return carry

    lax.fori_loop(0, slots, windows, 0)

    lane = lax.broadcasted_iota(jnp.int32, (BLK, HD), 1)

    def tag(s, carry):
        hit = lane == wid_s[s]
        at = pl.ds(pl.multiple_of(s * BLK, BLK), BLK)
        q_tag[at, :] = jnp.where(hit, 1.0, 0.0).astype(jnp.bfloat16)
        k_tag[at, :] = jnp.where(hit, 0.0, -FAR).astype(jnp.bfloat16)
        return carry

    lax.fori_loop(0, slots, tag, 0)
    scale = math.log2(math.e) / math.sqrt(HD)

    def attend(j, step):
        at = pl.ds(pl.multiple_of(step * rows, rows), rows)
        q = jnp.concatenate([recv[j, 0, at, :], q_tag[at, :]], axis=1)
        k = jnp.concatenate([recv[j, 1], k_tag[...]], axis=1)
        v = jnp.concatenate([recv[j, 2], jnp.ones((total, HD), jnp.bfloat16)], axis=1)
        scores = lax.dot_general(q, k, (((1,), (1,)), ((), ())), preferred_element_type=jnp.float32)
        row_max = jnp.max(scores, axis=1, keepdims=True)
        weights = jnp.exp2((scores - row_max) * scale).astype(jnp.bfloat16)
        both = jnp.dot(weights, v, preferred_element_type=jnp.float32)
        home[step, j, 0] = (both[:, :HD] / both[:, HD:]).astype(jnp.bfloat16)

    def gather(j, block, sem):
        for place in range(2, n_head, 2):
            gather_copy(j, block, place, sem.at[j]).start()
        gather_copy(j, block, 1, odd_sem.at[block]).start()

    def relay(j, block):
        for place in range(3, n_head, 2):
            relay_copy(j, block, place).start()

    def relay_near(j):
        if half > 1:
            arrived(home.at[pl.ds(0, late), j, pl.ds(1, half - 1)], near_sem.at[j])

        def body(i, carry):
            relay(j, late - 1 - i)
            return carry

        lax.fori_loop(0, late, body, 0)

    def relay_far(j):
        if half > 1:
            arrived(home.at[late, j, pl.ds(1, half - 1)], far_sem.at[j])
        relay(j, late)

    def project(block):
        arrived(home.at[block, :, pl.ds(half, half)], odd_sem.at[block])
        left = jnp.concatenate([home[block, j, p] for j in range(heads) for p in range(n_head)], axis=1)
        weight = wbuf[...].reshape(heads * n_head * HD, cols)
        term = jnp.dot(left, weight, preferred_element_type=jnp.float32)
        return term.reshape(cap, BLK, cols).astype(jnp.bfloat16)

    def attend_early(j, carry):
        kv_copy(j, 1, n_st - 1).wait_recv()
        if late > 1:
            q_copy(j, 1, late - 1).wait_recv()

        def body(i, c):
            attend(j, late - 1 - i)
            gather(j, late - 1 - i, near_sem)
            return c

        lax.fori_loop(0, late, body, 0)

        @pl.when(j >= 1)
        def _():
            relay_near(j - 1)

        return carry

    lax.fori_loop(0, heads, attend_early, 0)
    relay_near(heads - 1)

    own_weight.wait()
    weights_copy().wait()

    def give(block):
        ret_out[pl.ds(block * cap, cap)] = project(block)
        return_copy(block).start()

    for block in range(n_st - 2, 0, -1):
        give(block)

    def attend_late(j, carry):
        q_copy(j, late).wait_recv()
        attend(j, late)
        gather(j, late, far_sem)

        @pl.when(j >= LAG)
        def _():
            relay_far(j - LAG)

        return carry

    lax.fori_loop(0, heads, attend_late, 0)

    def relay_rest(j, carry):
        relay_far(j)
        return carry

    lax.fori_loop(max(heads - LAG, 0), heads, relay_rest, 0)
    give(late)
    ret_in[pl.ds(0, cap)] = project(0)

    away_copy().wait_send()
    others = home.at[:, :, pl.ds(1, n_head - 1)]
    head_copy(others, others, odd_sem.at[0], 1).wait_send()
    res_load.wait()
    return_copy(1, n_st - 1).wait()

    def put(t, carry):
        out_ref[t] = res_buf[t] + ret_in[slot_s[t]]
        return carry

    lax.fori_loop(0, tiles, put, 0)


def on_device(qkv_rows, out_weight, residual, source, target, window_first):
    tok_rows, three_way, feat_cols = qkv_rows.shape
    width = out_weight.shape[1]
    n_st = lax.axis_size("st")
    n_head = lax.axis_size("head")
    heads = feat_cols // HD
    cols = width // n_head
    tiles = tok_rows // BLK
    cap = max(2, (tiles + n_st - 1) // n_st)
    slots = n_st * cap
    total = slots * BLK
    rows = cap * BLK

    dims = (n_st, n_head, heads, tiles, cap, cols)
    bf16 = jnp.bfloat16
    i32 = jnp.int32
    dma = pltpu.SemaphoreType.DMA
    hbm = pl.BlockSpec(memory_space=pl.ANY)
    projected = pl.pallas_call(
        functools.partial(layer_kernel, dims),
        out_shape=pltpu.VMEM((tiles, BLK, cols), bf16),
        in_specs=[hbm] * 6,
        out_specs=pl.BlockSpec(memory_space=pltpu.VMEM),
        scratch_shapes=[
            pltpu.VMEM((3, tiles, BLK, HD), bf16),
            pltpu.VMEM((3, tiles, BLK, (heads - 1) * HD), bf16),
            pltpu.VMEM((heads, 3, total, HD), bf16),
            pltpu.VMEM((heads, 3, total, HD), bf16),
            pltpu.VMEM((n_st, heads, n_head, rows, HD), bf16),
            pltpu.VMEM((heads, n_head * HD, cols), bf16),
            pltpu.VMEM((total, HD), bf16),
            pltpu.VMEM((total, HD), bf16),
            pltpu.VMEM((tiles, BLK, cols), bf16),
            pltpu.VMEM((slots, BLK, cols), bf16),
            pltpu.VMEM((slots, BLK, cols), bf16),
            pltpu.SMEM((tok_rows,), i32),
            pltpu.SMEM((tok_rows,), i32),
            pltpu.SMEM((tok_rows,), i32),
            pltpu.SMEM((slots,), i32),
            pltpu.SMEM((2 * tiles,), i32),
            pltpu.SMEM((2 * tiles,), i32),
            pltpu.SMEM((slots,), i32),
            dma((2,)),
            dma((3,)),
            dma,
            dma,
            dma,
            dma((heads,)),
            dma((heads,)),
            dma((heads,)),
            dma,
            dma,
            dma,
            dma((heads,)),
            dma((heads,)),
            dma((n_st,)),
            dma,
            dma,
        ],
        compiler_params=pltpu.CompilerParams(
            collective_id=0, has_side_effects=True, vmem_limit_bytes=60 * 1024 * 1024
        ),
    )(
        source,
        target,
        window_first,
        jnp.transpose(qkv_rows, (1, 0, 2)).reshape(three_way, tiles, BLK, feat_cols),
        out_weight.reshape(heads, HD, width),
        residual.reshape(tiles, BLK, cols),
    )
    return projected.reshape(tok_rows, cols)


def solution(mesh):
    placed = (
        P(("group", "st"), None, "head"),
        P("head", None),
        P(("group", "st"), "head"),
        P(("group", "st")),
        P(("group", "st")),
        P(("group", "st")),
    )
    return jax.shard_map(
        on_device, mesh=mesh, in_specs=placed, out_specs=P(("group", "st"), "head"), check_vma=False
    )
```

```python
import functools
import math

import jax
import jax.numpy as jnp
from jax import lax
from jax.experimental import pallas as pl
from jax.experimental.pallas import tpu as pltpu
from jax.sharding import PartitionSpec as P

HD = 128
BLK = 64
FAR = 16384.0
LAG = 2
MESH = pl.DeviceIdType.MESH


def partner(a, b, n):
    total, bit = 0, 1
    while bit < n:
        total = total + ((a // bit + b // bit) % 2) * bit
        bit *= 2
    return total


def layer_kernel(
    dims,
    src_ref,
    tgt_ref,
    win_ref,
    qkv_ref,
    w_ref,
    res_ref,
    out_ref,
    first,
    rest,
    packed,
    recv,
    home,
    wbuf,
    q_tag,
    k_tag,
    res_buf,
    ret_out,
    ret_in,
    src_s,
    tgt_s,
    win_s,
    order_s,
    block_s,
    slot_s,
    wid_s,
    load_sem,
    idx_sem,
    wl_sem,
    res_sem,
    qs,
    kv_sem,
    early_sem,
    late_sem,
    rs,
    rr,
    gs,
    near_sem,
    far_sem,
    odd_sem,
    ws,
    wr,
):
    n_st, n_head, heads, tiles, cap, cols = dims
    rows = cap * BLK
    slots = n_st * cap
    total = n_st * rows
    tok_rows = tiles * BLK
    my_st = lax.axis_index("st")
    my_head = lax.axis_index("head")
    late = n_st - 1
    bits = (tiles - 1).bit_length()

    def st_peer(step):
        return {"st": partner(my_st, step, n_st)}

    def send_part(refs, sem, step):
        return pltpu.make_async_remote_copy(
            src_ref=refs[0],
            dst_ref=refs[1],
            send_sem=qs,
            recv_sem=sem,
            device_id=st_peer(step),
            device_id_type=MESH,
        )

    def kv_copy(j, step, count=1):
        at = (j, pl.ds(1, 2), pl.ds(step * rows, count * rows))
        return send_part((packed.at[at], recv.at[at]), kv_sem.at[j], step)

    def q_copy(j, step, count=1):
        at = (j, 0, pl.ds(step * rows, count * rows))
        sem = late_sem if step == late else early_sem.at[j]
        return send_part((packed.at[at], recv.at[at]), sem, step)

    def away_copy():
        at = (pl.ds(0, heads), pl.ds(0, 3), pl.ds(rows, total - rows))
        return send_part((packed.at[at], recv.at[at]), kv_sem.at[0], 1)

    def return_copy(step, count=1):
        part = pl.ds(step * cap, count * cap)
        return pltpu.make_async_remote_copy(
            src_ref=ret_out.at[part],
            dst_ref=ret_in.at[part],
            send_sem=rs,
            recv_sem=rr,
            device_id=st_peer(step),
            device_id_type=MESH,
        )

    chips = n_head // 2
    my_chip = my_head // 2
    my_core = lax.rem(my_head, 2)

    def head_of(place):
        chip = lax.rem(my_chip + place // 2, chips)
        core = my_core if place % 2 == 0 else 1 - my_core
        return chip * 2 + core

    half = n_head // 2

    def place_at(place):
        return place // 2 + half * (place % 2)

    def head_copy(source, dest, sem, place):
        return pltpu.make_async_remote_copy(
            src_ref=source,
            dst_ref=dest,
            send_sem=gs,
            recv_sem=sem,
            device_id={"head": head_of(place)},
            device_id_type=MESH,
        )

    def gather_copy(j, block, place, sem):
        return head_copy(home.at[block, j, 0], home.at[block, j, place_at(place)], sem, place)

    def relay_copy(j, block, place):
        return head_copy(
            home.at[block, j, place_at(place - 1)],
            home.at[block, j, place_at(place)],
            odd_sem.at[block],
            1,
        )

    def arrived(region, sem):
        head_copy(region, region, sem, 1).wait_recv()


    def weight_cols(place):
        return w_ref.at[:, :, pl.ds(pl.multiple_of(head_of(place) * cols, HD), cols)]

    def weight_copy(place):
        return pltpu.make_async_remote_copy(
            src_ref=weight_cols(place),
            dst_ref=wbuf.at[:, pl.ds(place_at(place) * HD, HD), :],
            send_sem=ws,
            recv_sem=wr,
            device_id={"head": head_of(place)},
            device_id_type=MESH,
        )

    def weights_copy():
        others = wbuf.at[:, pl.ds(HD, (n_head - 1) * HD), :]
        return pltpu.make_async_remote_copy(
            src_ref=others,
            dst_ref=others,
            send_sem=ws,
            recv_sem=wr,
            device_id={"head": head_of(1)},
            device_id_type=MESH,
        )

    own_weight = pltpu.make_async_copy(weight_cols(0), wbuf.at[:, pl.ds(0, HD), :], wl_sem)
    res_load = pltpu.make_async_copy(res_ref, res_buf, res_sem)
    tgt_load = pltpu.make_async_copy(tgt_ref, tgt_s, idx_sem.at[0])
    src_load = pltpu.make_async_copy(src_ref, src_s, idx_sem.at[1])
    win_load = pltpu.make_async_copy(win_ref, win_s, idx_sem.at[2])
    first_load = pltpu.make_async_copy(qkv_ref.at[:, :, :, pl.ds(0, HD)], first, load_sem.at[0])
    rest_load = pltpu.make_async_copy(
        qkv_ref.at[:, :, :, pl.ds(HD, (heads - 1) * HD)], rest, load_sem.at[1]
    )

    tgt_load.start()
    first_load.start()

    barrier = pltpu.get_barrier_semaphore()
    for step in range(1, n_st):
        pl.semaphore_signal(barrier, inc=1, device_id=st_peer(step), device_id_type=MESH)
    for step in range(1, n_head):
        pl.semaphore_signal(barrier, inc=1, device_id={"head": head_of(step)}, device_id_type=MESH)

    rest_load.start()
    src_load.start()
    win_load.start()
    own_weight.start()
    res_load.start()

    tgt_load.wait()

    def list_tiles(step, carry):
        low = partner(my_st, step, n_st) * tok_rows
        found = jnp.int32(0)
        for i in reversed(range(tiles)):
            at = tgt_s[i * BLK]
            found = jnp.where((at >= low) & (at < low + tok_rows), (found << bits) + i, found)
        for r in range(cap):
            order_s[step * cap + r] = (found >> (bits * r)) & ((1 << bits) - 1)
        return carry

    lax.fori_loop(0, n_st, list_tiles, 0)

    def pack_first(s, carry):
        tile = order_s[s]
        at = pl.ds(pl.multiple_of(s * BLK, BLK), BLK)
        for part in range(3):
            packed[0, part, at, :] = first[part, tile]
        return carry

    def pack_rest(j, s):
        tile = order_s[s]
        at = pl.ds(pl.multiple_of(s * BLK, BLK), BLK)
        lanes = pl.ds(pl.multiple_of((j - 1) * HD, HD), HD)
        for part in range(3):
            packed[j, part, at, :] = rest[part, tile, :, lanes]

    across = list(range(n_st - 1, 0, -1))

    first_load.wait()
    pl.semaphore_wait(barrier, n_st + n_head - 2)
    for step in across:
        lax.fori_loop(step * cap, (step + 1) * cap, pack_first, 0)
        kv_copy(0, step).start()
        if step != late:
            q_copy(0, step).start()

    def own_first(s, carry):
        tile = order_s[s]
        at = pl.ds(pl.multiple_of(s * BLK, BLK), BLK)
        for part in range(3):
            recv[0, part, at, :] = first[part, tile]
        return carry

    lax.fori_loop(0, cap, own_first, 0)
    rest_load.wait()

    def dispatch(j, carry):
        for step in across:

            def body(s, c):
                pack_rest(j, s)
                return c

            lax.fori_loop(step * cap, (step + 1) * cap, body, 0)
            kv_copy(j, step).start()
            if step != late:
                q_copy(j, step).start()

        def own(s, c):
            tile = order_s[s]
            at = pl.ds(pl.multiple_of(s * BLK, BLK), BLK)
            lanes = pl.ds(pl.multiple_of((j - 1) * HD, HD), HD)
            for part in range(3):
                recv[j, part, at, :] = rest[part, tile, :, lanes]
            return c

        lax.fori_loop(0, cap, own, 0)
        return carry

    lax.fori_loop(1, heads, dispatch, 0)

    def send_late(j, carry):
        q_copy(j, late).start()
        return carry

    lax.fori_loop(0, heads, send_late, 0)
    for place in range(1, n_head):
        weight_copy(place).start()

    def block_of(value):
        found = jnp.int32(0)
        for b in range(1, n_st):
            found = found + (value >= b * tok_rows).astype(jnp.int32)
        return found

    def own_slots(i, carry):
        block_s[i] = block_of(tgt_s[i * BLK])
        return carry

    lax.fori_loop(0, tiles, own_slots, 0)

    def send_slots(i, carry):
        mine = block_s[i]
        rank = jnp.int32(0)
        for other in range(tiles):
            rank = rank + ((block_s[other] == mine) & (other < i)).astype(jnp.int32)
        slot_s[i] = partner(my_st, mine, n_st) * cap + jnp.minimum(rank, cap - 1)
        return carry

    lax.fori_loop(0, tiles, send_slots, 0)
    src_load.wait()
    win_load.wait()

    def away_blocks(i, carry):
        block_s[tiles + i] = block_of(src_s[i * BLK])
        return carry

    lax.fori_loop(0, tiles, away_blocks, 0)

    def recv_slots(i, carry):
        mine = block_s[tiles + i]
        rank = jnp.int32(0)
        for other in range(tiles):
            rank = rank + (
                (block_s[tiles + other] == mine) & (src_s[other * BLK] < src_s[i * BLK])
            ).astype(jnp.int32)
        slot_s[tiles + i] = partner(my_st, mine, n_st) * cap + jnp.minimum(rank, cap - 1)
        return carry

    lax.fori_loop(0, tiles, recv_slots, 0)

    def windows(s, carry):
        found = jnp.int32((HD - 1) * BLK) + my_st * tok_rows
        for i in range(tiles):
            found = jnp.where(slot_s[tiles + i] == s, win_s[i * BLK], found)
        wid_s[s] = (found - my_st * tok_rows) >> (BLK.bit_length() - 1)
        return carry

    lax.fori_loop(0, slots, windows, 0)

    lane = lax.broadcasted_iota(jnp.int32, (BLK, HD), 1)

    def tag(s, carry):
        hit = lane == wid_s[s]
        at = pl.ds(pl.multiple_of(s * BLK, BLK), BLK)
        q_tag[at, :] = jnp.where(hit, 1.0, 0.0).astype(jnp.bfloat16)
        k_tag[at, :] = jnp.where(hit, 0.0, -FAR).astype(jnp.bfloat16)
        return carry

    lax.fori_loop(0, slots, tag, 0)
    scale = math.log2(math.e) / math.sqrt(HD)

    def attend(j, step):
        at = pl.ds(pl.multiple_of(step * rows, rows), rows)
        q = jnp.concatenate([recv[j, 0, at, :], q_tag[at, :]], axis=1)
        k = jnp.concatenate([recv[j, 1], k_tag[...]], axis=1)
        v = jnp.concatenate([recv[j, 2], jnp.ones((total, HD), jnp.bfloat16)], axis=1)
        scores = lax.dot_general(q, k, (((1,), (1,)), ((), ())), preferred_element_type=jnp.float32)
        row_max = jnp.max(scores, axis=1, keepdims=True)
        weights = jnp.exp2((scores - row_max) * scale).astype(jnp.bfloat16)
        both = jnp.dot(weights, v, preferred_element_type=jnp.float32)
        home[step, j, 0] = (both[:, :HD] / both[:, HD:]).astype(jnp.bfloat16)

    def gather(j, block, sem):
        for place in range(2, n_head, 2):
            gather_copy(j, block, place, sem.at[j]).start()
        gather_copy(j, block, 1, odd_sem.at[block]).start()

    def relay(j, block):
        for place in range(3, n_head, 2):
            relay_copy(j, block, place).start()

    def relay_near(j):
        if half > 1:
            arrived(home.at[pl.ds(0, late), j, pl.ds(1, half - 1)], near_sem.at[j])

        def body(i, carry):
            relay(j, late - 1 - i)
            return carry

        lax.fori_loop(0, late, body, 0)

    def relay_far(j):
        if half > 1:
            arrived(home.at[late, j, pl.ds(1, half - 1)], far_sem.at[j])
        relay(j, late)

    def project(block):
        arrived(home.at[block, :, pl.ds(half, half)], odd_sem.at[block])
        left = jnp.concatenate([home[block, j, p] for j in range(heads) for p in range(n_head)], axis=1)
        weight = wbuf[...].reshape(heads * n_head * HD, cols)
        term = jnp.dot(left, weight, preferred_element_type=jnp.float32)
        return term.reshape(cap, BLK, cols).astype(jnp.bfloat16)

    def attend_early(j, carry):
        kv_copy(j, 1, n_st - 1).wait_recv()
        if late > 1:
            q_copy(j, 1, late - 1).wait_recv()

        def body(i, c):
            attend(j, late - 1 - i)
            gather(j, late - 1 - i, near_sem)
            return c

        lax.fori_loop(0, late, body, 0)

        @pl.when(j >= 1)
        def _():
            relay_near(j - 1)

        return carry

    lax.fori_loop(0, heads, attend_early, 0)
    relay_near(heads - 1)

    own_weight.wait()
    weights_copy().wait()

    def give(block):
        ret_out[pl.ds(block * cap, cap)] = project(block)
        return_copy(block).start()

    for block in range(n_st - 2, 0, -1):
        give(block)

    last = (pl.ds(0, heads), 0, pl.ds(late * rows, rows))
    send_part((packed.at[last], recv.at[last]), late_sem, late).wait_recv()

    def attend_late(j, carry):
        attend(j, late)
        gather(j, late, far_sem)

        @pl.when(j >= LAG)
        def _():
            relay_far(j - LAG)

        return carry

    lax.fori_loop(0, heads, attend_late, 0)

    def relay_rest(j, carry):
        relay_far(j)
        return carry

    lax.fori_loop(max(heads - LAG, 0), heads, relay_rest, 0)
    give(late)
    ret_in[pl.ds(0, cap)] = project(0)

    away_copy().wait_send()
    others = home.at[:, :, pl.ds(1, n_head - 1)]
    head_copy(others, others, odd_sem.at[0], 1).wait_send()
    res_load.wait()
    return_copy(1, n_st - 1).wait()

    def put(t, carry):
        out_ref[t] = res_buf[t] + ret_in[slot_s[t]]
        return carry

    lax.fori_loop(0, tiles, put, 0)


def on_device(qkv_rows, out_weight, residual, source, target, window_first):
    tok_rows, three_way, feat_cols = qkv_rows.shape
    width = out_weight.shape[1]
    n_st = lax.axis_size("st")
    n_head = lax.axis_size("head")
    heads = feat_cols // HD
    cols = width // n_head
    tiles = tok_rows // BLK
    cap = max(2, (tiles + n_st - 1) // n_st)
    slots = n_st * cap
    total = slots * BLK
    rows = cap * BLK

    dims = (n_st, n_head, heads, tiles, cap, cols)
    bf16 = jnp.bfloat16
    i32 = jnp.int32
    dma = pltpu.SemaphoreType.DMA
    hbm = pl.BlockSpec(memory_space=pl.ANY)
    projected = pl.pallas_call(
        functools.partial(layer_kernel, dims),
        out_shape=pltpu.VMEM((tiles, BLK, cols), bf16),
        in_specs=[hbm] * 6,
        out_specs=pl.BlockSpec(memory_space=pltpu.VMEM),
        scratch_shapes=[
            pltpu.VMEM((3, tiles, BLK, HD), bf16),
            pltpu.VMEM((3, tiles, BLK, (heads - 1) * HD), bf16),
            pltpu.VMEM((heads, 3, total, HD), bf16),
            pltpu.VMEM((heads, 3, total, HD), bf16),
            pltpu.VMEM((n_st, heads, n_head, rows, HD), bf16),
            pltpu.VMEM((heads, n_head * HD, cols), bf16),
            pltpu.VMEM((total, HD), bf16),
            pltpu.VMEM((total, HD), bf16),
            pltpu.VMEM((tiles, BLK, cols), bf16),
            pltpu.VMEM((slots, BLK, cols), bf16),
            pltpu.VMEM((slots, BLK, cols), bf16),
            pltpu.SMEM((tok_rows,), i32),
            pltpu.SMEM((tok_rows,), i32),
            pltpu.SMEM((tok_rows,), i32),
            pltpu.SMEM((slots,), i32),
            pltpu.SMEM((2 * tiles,), i32),
            pltpu.SMEM((2 * tiles,), i32),
            pltpu.SMEM((slots,), i32),
            dma((2,)),
            dma((3,)),
            dma,
            dma,
            dma,
            dma((heads,)),
            dma((heads,)),
            dma,
            dma,
            dma,
            dma,
            dma((heads,)),
            dma((heads,)),
            dma((n_st,)),
            dma,
            dma,
        ],
        compiler_params=pltpu.CompilerParams(
            collective_id=0, has_side_effects=True, vmem_limit_bytes=60 * 1024 * 1024
        ),
    )(
        source,
        target,
        window_first,
        jnp.transpose(qkv_rows, (1, 0, 2)).reshape(three_way, tiles, BLK, feat_cols),
        out_weight.reshape(heads, HD, width),
        residual.reshape(tiles, BLK, cols),
    )
    return projected.reshape(tok_rows, cols)


def solution(mesh):
    placed = (
        P(("group", "st"), None, "head"),
        P("head", None),
        P(("group", "st"), "head"),
        P(("group", "st")),
        P(("group", "st")),
        P(("group", "st")),
    )
    return jax.shard_map(
        on_device, mesh=mesh, in_specs=placed, out_specs=P(("group", "st"), "head"), check_vma=False
    )
```

```python
import functools
import math

import jax
import jax.numpy as jnp
from jax import lax
from jax.experimental import pallas as pl
from jax.experimental.pallas import tpu as pltpu
from jax.sharding import PartitionSpec as P

HD = 128
BLK = 64
FAR = 16384.0
LAG = 2
MESH = pl.DeviceIdType.MESH


def partner(a, b, n):
    total, bit = 0, 1
    while bit < n:
        total = total + ((a // bit + b // bit) % 2) * bit
        bit *= 2
    return total


def layer_kernel(
    dims,
    src_ref,
    tgt_ref,
    win_ref,
    qkv_ref,
    w_ref,
    res_ref,
    out_ref,
    first,
    rest,
    packed,
    recv,
    home,
    wbuf,
    q_tag,
    k_tag,
    res_buf,
    ret_out,
    ret_in,
    src_s,
    tgt_s,
    win_s,
    order_s,
    block_s,
    slot_s,
    wid_s,
    load_sem,
    idx_sem,
    wl_sem,
    res_sem,
    qs,
    kv_sem,
    early_sem,
    late_sem,
    rs,
    rr,
    gs,
    near_sem,
    far_sem,
    odd_sem,
    ws,
    wr,
):
    n_st, n_head, heads, tiles, cap, cols = dims
    rows = cap * BLK
    slots = n_st * cap
    total = n_st * rows
    tok_rows = tiles * BLK
    my_st = lax.axis_index("st")
    my_head = lax.axis_index("head")
    late = n_st - 1
    bits = (tiles - 1).bit_length()

    def st_peer(step):
        return {"st": partner(my_st, step, n_st)}

    def send_part(refs, sem, step):
        return pltpu.make_async_remote_copy(
            src_ref=refs[0],
            dst_ref=refs[1],
            send_sem=qs,
            recv_sem=sem,
            device_id=st_peer(step),
            device_id_type=MESH,
        )

    def kv_copy(j, step, count=1):
        at = (j, pl.ds(1, 2), pl.ds(step * rows, count * rows))
        return send_part((packed.at[at], recv.at[at]), kv_sem.at[j], step)

    def q_copy(j, step, count=1):
        at = (j, 0, pl.ds(step * rows, count * rows))
        sem = late_sem if step == late else early_sem
        return send_part((packed.at[at], recv.at[at]), sem.at[j], step)

    def away_copy():
        at = (pl.ds(0, heads), pl.ds(0, 3), pl.ds(rows, total - rows))
        return send_part((packed.at[at], recv.at[at]), kv_sem.at[0], 1)

    def return_copy(step, count=1):
        part = pl.ds(step * cap, count * cap)
        return pltpu.make_async_remote_copy(
            src_ref=ret_out.at[part],
            dst_ref=ret_in.at[part],
            send_sem=rs,
            recv_sem=rr,
            device_id=st_peer(step),
            device_id_type=MESH,
        )

    chips = n_head // 2
    my_chip = my_head // 2
    my_core = lax.rem(my_head, 2)

    def head_of(place):
        chip = lax.rem(my_chip + place // 2, chips)
        core = my_core if place % 2 == 0 else 1 - my_core
        return chip * 2 + core

    half = n_head // 2

    def place_at(place):
        return place // 2 + half * (place % 2)

    def head_copy(source, dest, sem, place):
        return pltpu.make_async_remote_copy(
            src_ref=source,
            dst_ref=dest,
            send_sem=gs,
            recv_sem=sem,
            device_id={"head": head_of(place)},
            device_id_type=MESH,
        )

    def gather_copy(j, block, place, sem):
        return head_copy(home.at[block, j, 0], home.at[block, j, place_at(place)], sem, place)

    def relay_copy(j, block, place):
        return head_copy(
            home.at[block, j, place_at(place - 1)],
            home.at[block, j, place_at(place)],
            odd_sem.at[block],
            1,
        )

    def arrived(region, sem):
        head_copy(region, region, sem, 1).wait_recv()


    def weight_cols(place):
        return w_ref.at[:, :, pl.ds(pl.multiple_of(head_of(place) * cols, HD), cols)]

    def weight_copy(place):
        return pltpu.make_async_remote_copy(
            src_ref=weight_cols(place),
            dst_ref=wbuf.at[:, pl.ds(place_at(place) * HD, HD), :],
            send_sem=ws,
            recv_sem=wr,
            device_id={"head": head_of(place)},
            device_id_type=MESH,
        )

    def weights_copy():
        others = wbuf.at[:, pl.ds(HD, (n_head - 1) * HD), :]
        return pltpu.make_async_remote_copy(
            src_ref=others,
            dst_ref=others,
            send_sem=ws,
            recv_sem=wr,
            device_id={"head": head_of(1)},
            device_id_type=MESH,
        )

    own_weight = pltpu.make_async_copy(weight_cols(0), wbuf.at[:, pl.ds(0, HD), :], wl_sem)
    res_load = pltpu.make_async_copy(res_ref, res_buf, res_sem)
    tgt_load = pltpu.make_async_copy(tgt_ref, tgt_s, idx_sem.at[0])
    src_load = pltpu.make_async_copy(src_ref, src_s, idx_sem.at[1])
    win_load = pltpu.make_async_copy(win_ref, win_s, idx_sem.at[2])
    first_load = pltpu.make_async_copy(qkv_ref.at[:, :, :, pl.ds(0, HD)], first, load_sem.at[0])
    rest_load = pltpu.make_async_copy(
        qkv_ref.at[:, :, :, pl.ds(HD, (heads - 1) * HD)], rest, load_sem.at[1]
    )

    barrier = pltpu.get_barrier_semaphore()
    for step in range(1, n_st):
        pl.semaphore_signal(barrier, inc=1, device_id=st_peer(step), device_id_type=MESH)
    for step in range(1, n_head):
        pl.semaphore_signal(barrier, inc=1, device_id={"head": head_of(step)}, device_id_type=MESH)

    tgt_load.start()
    first_load.start()

    rest_load.start()
    src_load.start()
    win_load.start()
    own_weight.start()
    res_load.start()

    tgt_load.wait()

    def list_tiles(step, carry):
        low = partner(my_st, step, n_st) * tok_rows
        found = jnp.int32(0)
        for i in reversed(range(tiles)):
            at = tgt_s[i * BLK]
            found = jnp.where((at >= low) & (at < low + tok_rows), (found << bits) + i, found)
        for r in range(cap):
            order_s[step * cap + r] = (found >> (bits * r)) & ((1 << bits) - 1)
        return carry

    lax.fori_loop(0, n_st, list_tiles, 0)

    def pack_first(s, carry):
        tile = order_s[s]
        at = pl.ds(pl.multiple_of(s * BLK, BLK), BLK)
        for part in range(3):
            packed[0, part, at, :] = first[part, tile]
        return carry

    def pack_rest(j, s):
        tile = order_s[s]
        at = pl.ds(pl.multiple_of(s * BLK, BLK), BLK)
        lanes = pl.ds(pl.multiple_of((j - 1) * HD, HD), HD)
        for part in range(3):
            packed[j, part, at, :] = rest[part, tile, :, lanes]

    across = list(range(n_st - 1, 0, -1))

    first_load.wait()
    pl.semaphore_wait(barrier, n_st + n_head - 2)
    for step in across:
        lax.fori_loop(step * cap, (step + 1) * cap, pack_first, 0)
        kv_copy(0, step).start()
        if step != late:
            q_copy(0, step).start()

    def own_first(s, carry):
        tile = order_s[s]
        at = pl.ds(pl.multiple_of(s * BLK, BLK), BLK)
        for part in range(3):
            recv[0, part, at, :] = first[part, tile]
        return carry

    lax.fori_loop(0, cap, own_first, 0)
    rest_load.wait()

    def dispatch(j, carry):
        for step in across:

            def body(s, c):
                pack_rest(j, s)
                return c

            lax.fori_loop(step * cap, (step + 1) * cap, body, 0)
            kv_copy(j, step).start()
            if step != late:
                q_copy(j, step).start()

        def own(s, c):
            tile = order_s[s]
            at = pl.ds(pl.multiple_of(s * BLK, BLK), BLK)
            lanes = pl.ds(pl.multiple_of((j - 1) * HD, HD), HD)
            for part in range(3):
                recv[j, part, at, :] = rest[part, tile, :, lanes]
            return c

        lax.fori_loop(0, cap, own, 0)
        return carry

    lax.fori_loop(1, heads, dispatch, 0)

    def send_late(j, carry):
        q_copy(j, late).start()
        return carry

    lax.fori_loop(0, heads, send_late, 0)
    for place in range(1, n_head):
        weight_copy(place).start()

    def block_of(value):
        found = jnp.int32(0)
        for b in range(1, n_st):
            found = found + (value >= b * tok_rows).astype(jnp.int32)
        return found

    def own_slots(i, carry):
        block_s[i] = block_of(tgt_s[i * BLK])
        return carry

    lax.fori_loop(0, tiles, own_slots, 0)

    def send_slots(i, carry):
        mine = block_s[i]
        rank = jnp.int32(0)
        for other in range(tiles):
            rank = rank + ((block_s[other] == mine) & (other < i)).astype(jnp.int32)
        slot_s[i] = partner(my_st, mine, n_st) * cap + jnp.minimum(rank, cap - 1)
        return carry

    lax.fori_loop(0, tiles, send_slots, 0)
    src_load.wait()
    win_load.wait()

    def away_blocks(i, carry):
        block_s[tiles + i] = block_of(src_s[i * BLK])
        return carry

    lax.fori_loop(0, tiles, away_blocks, 0)

    def recv_slots(i, carry):
        mine = block_s[tiles + i]
        rank = jnp.int32(0)
        for other in range(tiles):
            rank = rank + (
                (block_s[tiles + other] == mine) & (src_s[other * BLK] < src_s[i * BLK])
            ).astype(jnp.int32)
        slot_s[tiles + i] = partner(my_st, mine, n_st) * cap + jnp.minimum(rank, cap - 1)
        return carry

    lax.fori_loop(0, tiles, recv_slots, 0)

    def windows(s, carry):
        found = jnp.int32((HD - 1) * BLK) + my_st * tok_rows
        for i in range(tiles):
            found = jnp.where(slot_s[tiles + i] == s, win_s[i * BLK], found)
        wid_s[s] = (found - my_st * tok_rows) >> (BLK.bit_length() - 1)
        return carry

    lax.fori_loop(0, slots, windows, 0)

    lane = lax.broadcasted_iota(jnp.int32, (BLK, HD), 1)

    def tag(s, carry):
        hit = lane == wid_s[s]
        at = pl.ds(pl.multiple_of(s * BLK, BLK), BLK)
        q_tag[at, :] = jnp.where(hit, 1.0, 0.0).astype(jnp.bfloat16)
        k_tag[at, :] = jnp.where(hit, 0.0, -FAR).astype(jnp.bfloat16)
        return carry

    lax.fori_loop(0, slots, tag, 0)
    scale = math.log2(math.e) / math.sqrt(HD)

    def attend(j, step):
        at = pl.ds(pl.multiple_of(step * rows, rows), rows)
        q = jnp.concatenate([recv[j, 0, at, :], q_tag[at, :]], axis=1)
        k = jnp.concatenate([recv[j, 1], k_tag[...]], axis=1)
        v = jnp.concatenate([recv[j, 2], jnp.ones((total, HD), jnp.bfloat16)], axis=1)
        scores = lax.dot_general(q, k, (((1,), (1,)), ((), ())), preferred_element_type=jnp.float32)
        row_max = jnp.max(scores, axis=1, keepdims=True)
        weights = jnp.exp2((scores - row_max) * scale).astype(jnp.bfloat16)
        both = jnp.dot(weights, v, preferred_element_type=jnp.float32)
        home[step, j, 0] = (both[:, :HD] / both[:, HD:]).astype(jnp.bfloat16)

    def gather(j, block, sem):
        for place in range(2, n_head, 2):
            gather_copy(j, block, place, sem.at[j]).start()
        gather_copy(j, block, 1, odd_sem.at[block]).start()

    def relay(j, block):
        for place in range(3, n_head, 2):
            relay_copy(j, block, place).start()

    def relay_near(j):
        if half > 1:
            arrived(home.at[pl.ds(0, late), j, pl.ds(1, half - 1)], near_sem.at[j])

        def body(i, carry):
            relay(j, late - 1 - i)
            return carry

        lax.fori_loop(0, late, body, 0)

    def relay_far(j):
        if half > 1:
            arrived(home.at[late, j, pl.ds(1, half - 1)], far_sem.at[j])
        relay(j, late)

    def project(block):
        arrived(home.at[block, :, pl.ds(half, half)], odd_sem.at[block])
        left = jnp.concatenate([home[block, j, p] for j in range(heads) for p in range(n_head)], axis=1)
        weight = wbuf[...].reshape(heads * n_head * HD, cols)
        term = jnp.dot(left, weight, preferred_element_type=jnp.float32)
        return term.reshape(cap, BLK, cols).astype(jnp.bfloat16)

    def attend_early(j, carry):
        kv_copy(j, 1, n_st - 1).wait_recv()
        if late > 1:
            q_copy(j, 1, late - 1).wait_recv()

        def body(i, c):
            attend(j, late - 1 - i)
            gather(j, late - 1 - i, near_sem)
            return c

        lax.fori_loop(0, late, body, 0)

        @pl.when(j >= 1)
        def _():
            relay_near(j - 1)

        return carry

    lax.fori_loop(0, heads, attend_early, 0)
    relay_near(heads - 1)

    own_weight.wait()
    weights_copy().wait()

    def give(block):
        ret_out[pl.ds(block * cap, cap)] = project(block)
        return_copy(block).start()

    for block in range(n_st - 2, 0, -1):
        give(block)

    def attend_late(j, carry):
        q_copy(j, late).wait_recv()
        attend(j, late)
        gather(j, late, far_sem)

        @pl.when(j >= LAG)
        def _():
            relay_far(j - LAG)

        return carry

    lax.fori_loop(0, heads, attend_late, 0)

    def relay_rest(j, carry):
        relay_far(j)
        return carry

    lax.fori_loop(max(heads - LAG, 0), heads, relay_rest, 0)
    give(late)
    ret_in[pl.ds(0, cap)] = project(0)

    away_copy().wait_send()
    others = home.at[:, :, pl.ds(1, n_head - 1)]
    head_copy(others, others, odd_sem.at[0], 1).wait_send()
    res_load.wait()
    return_copy(1, n_st - 1).wait()

    def put(t, carry):
        out_ref[t] = res_buf[t] + ret_in[slot_s[t]]
        return carry

    lax.fori_loop(0, tiles, put, 0)


def on_device(qkv_rows, out_weight, residual, source, target, window_first):
    tok_rows, three_way, feat_cols = qkv_rows.shape
    width = out_weight.shape[1]
    n_st = lax.axis_size("st")
    n_head = lax.axis_size("head")
    heads = feat_cols // HD
    cols = width // n_head
    tiles = tok_rows // BLK
    cap = max(2, (tiles + n_st - 1) // n_st)
    slots = n_st * cap
    total = slots * BLK
    rows = cap * BLK

    dims = (n_st, n_head, heads, tiles, cap, cols)
    bf16 = jnp.bfloat16
    i32 = jnp.int32
    dma = pltpu.SemaphoreType.DMA
    hbm = pl.BlockSpec(memory_space=pl.ANY)
    projected = pl.pallas_call(
        functools.partial(layer_kernel, dims),
        out_shape=pltpu.VMEM((tiles, BLK, cols), bf16),
        in_specs=[hbm] * 6,
        out_specs=pl.BlockSpec(memory_space=pltpu.VMEM),
        scratch_shapes=[
            pltpu.VMEM((3, tiles, BLK, HD), bf16),
            pltpu.VMEM((3, tiles, BLK, (heads - 1) * HD), bf16),
            pltpu.VMEM((heads, 3, total, HD), bf16),
            pltpu.VMEM((heads, 3, total, HD), bf16),
            pltpu.VMEM((n_st, heads, n_head, rows, HD), bf16),
            pltpu.VMEM((heads, n_head * HD, cols), bf16),
            pltpu.VMEM((total, HD), bf16),
            pltpu.VMEM((total, HD), bf16),
            pltpu.VMEM((tiles, BLK, cols), bf16),
            pltpu.VMEM((slots, BLK, cols), bf16),
            pltpu.VMEM((slots, BLK, cols), bf16),
            pltpu.SMEM((tok_rows,), i32),
            pltpu.SMEM((tok_rows,), i32),
            pltpu.SMEM((tok_rows,), i32),
            pltpu.SMEM((slots,), i32),
            pltpu.SMEM((2 * tiles,), i32),
            pltpu.SMEM((2 * tiles,), i32),
            pltpu.SMEM((slots,), i32),
            dma((2,)),
            dma((3,)),
            dma,
            dma,
            dma,
            dma((heads,)),
            dma((heads,)),
            dma((heads,)),
            dma,
            dma,
            dma,
            dma((heads,)),
            dma((heads,)),
            dma((n_st,)),
            dma,
            dma,
        ],
        compiler_params=pltpu.CompilerParams(
            collective_id=0, has_side_effects=True, vmem_limit_bytes=60 * 1024 * 1024
        ),
    )(
        source,
        target,
        window_first,
        jnp.transpose(qkv_rows, (1, 0, 2)).reshape(three_way, tiles, BLK, feat_cols),
        out_weight.reshape(heads, HD, width),
        residual.reshape(tiles, BLK, cols),
    )
    return projected.reshape(tok_rows, cols)


def solution(mesh):
    placed = (
        P(("group", "st"), None, "head"),
        P("head", None),
        P(("group", "st"), "head"),
        P(("group", "st")),
        P(("group", "st")),
        P(("group", "st")),
    )
    return jax.shard_map(
        on_device, mesh=mesh, in_specs=placed, out_specs=P(("group", "st"), "head"), check_vma=False
    )
```
